512 devices in a mesh: samp: 64 (over z, y), hour: 8 (over x, core).
Axes of the slice: x: 4, y: 4, z: 16, core: 2. Of those that a mesh axis runs over, the one named last changes fastest.
Arguments:
- load_gap: float32 [3008, 4, 256], P('samp', None, 'hour'), may hold values from -21 to 21
- profiles: bfloat16 [4, 256, 131072], P(None, 'hour', 'samp'), may hold values from 0.019897461 to 0.3984375
- slot_of_sample: int32 [131072], P('samp'), may hold values from 0 to 1023, as said below
- slot_county: int32 [64, 1024], replicated, may hold values from 0 to 3007, as said below
Outputs:
- weight_step: float32 [4, 131072], P(None, ('samp', 'hour'))
- search_dir: float32 [4, 131072], P(None, ('samp', 'hour'))
- load_dir: float32 [3008, 4, 256], P('samp', None, 'hour')
The draws below stay inside these ranges and needn't reach their ends.
Inputs may be any that keep to these rules, and one draw needn't show every extreme that they name: `slot_of_sample`: every slot 0 to 1023 of an index of samp is used by some sample of that index. `slot_county`: row d lists 1024 distinct counties in increasing order; county c is owned by index c // 47 of samp. At most 32 counties of a row have one owner; in every draw some owner has exactly 32 counties in every row.
All inputs are finite; a program needn't handle non-finite values.
Results may differ from the reference program's by a relative error of at most 0.00062.
Values sent between devices are 32-bit elements; how exact they have to be, the bound alone decides.
A program may use at most 64 MiB of HBM per device.

```python
import math
import jax
import jax.numpy as jnp
from jax import lax

USES = 4
SAMP_DEV = 2048
C_DEV = 47
CAP = 32
LOCAL = 1024
HOURS = 256
SAMPLES = 131072
COUNTIES = 3008
N_SAMP = 64


def draw_load_gap(key, part):
    county_frac = jnp.arange(COUNTIES, dtype=jnp.float32) / COUNTIES
    hour_frac = jnp.arange(HOURS, dtype=jnp.float32) / HOURS
    base_values = jnp.clip(jax.random.normal(key, (COUNTIES, USES, HOURS), jnp.float32), -4.0, 4.0)
    ramp_scale = jnp.exp(jnp.log(3.0) * county_frac)[:, None, None] * jnp.exp(jnp.log(1.7) * hour_frac)[None, None, :]
    return base_values * ramp_scale


def draw_slot_of_sample(key, part):
    key_list = jax.random.split(key, N_SAMP + 1)
    filler = jax.random.randint(key_list[0], (N_SAMP, SAMP_DEV - LOCAL), 0, LOCAL, dtype=jnp.int32)
    firsts = jax.vmap(lambda subkey: jax.random.permutation(subkey, LOCAL))(key_list[1:]).astype(jnp.int32)
    return jnp.concatenate([firsts, filler], axis=1).reshape(N_SAMP * SAMP_DEV)


def draw_slot_county(key, part):
    key_full, key_pairs, key_order, key_pick = jax.random.split(key, 4)
    half_cap = CAP // 2
    full_owner = jax.random.randint(key_full, (), 0, N_SAMP, dtype=jnp.int32)
    shifts = jax.random.randint(key_pairs, (N_SAMP, N_SAMP // 2), 0, half_cap + 1, dtype=jnp.int32)
    shifts = shifts.at[:, 0].set(half_cap)
    order_keys = jax.random.split(key_order, N_SAMP)
    rest_order = jax.vmap(lambda subkey: jax.random.permutation(subkey, N_SAMP - 1))(order_keys).astype(jnp.int32)
    owner_order = jnp.concatenate([jnp.zeros((N_SAMP, 1), jnp.int32), rest_order + 1], axis=1)
    owner_order = (owner_order + full_owner) % N_SAMP
    counts_pos = jnp.stack([half_cap + shifts, half_cap - shifts], axis=2).reshape(N_SAMP, N_SAMP)
    owner_index = jnp.arange(N_SAMP, dtype=jnp.int32)
    counts = jnp.sum(jnp.where(owner_order[:, :, None] == owner_index[None, None, :], counts_pos[:, :, None], 0), axis=1)
    pick_keys = jax.random.split(key_pick, N_SAMP * N_SAMP)
    ranks = jax.vmap(lambda subkey: jax.random.permutation(subkey, C_DEV))(pick_keys).astype(jnp.int32)
    ranks = ranks.reshape(N_SAMP, N_SAMP, C_DEV)
    chosen = (ranks < counts[:, :, None]).reshape(N_SAMP, COUNTIES)
    county_index = jnp.arange(COUNTIES, dtype=jnp.int32)
    scores = jnp.where(chosen, COUNTIES - county_index[None, :], -1 - county_index[None, :])
    top_scores, _ = lax.top_k(scores, LOCAL)
    return (COUNTIES - top_scores).astype(jnp.int32)


def block_scale(key, extent, shards, least, largest):
    def one(axis_at, shards_of):
        steps = jax.random.uniform(jax.random.fold_in(jax.random.fold_in(key, 6), axis_at), (shards_of,), jnp.float32, least / len(shards), largest / len(shards))
        return jnp.repeat(jnp.exp(steps), extent[axis_at] // shards_of).reshape((-1,) + (1,) * (len(extent) - axis_at - 1))

    gain = one(*shards[0])
    for cut in shards[1:]:
        gain = gain * one(*cut)
    return gain


def setup_inputs(seed: int = 0) -> dict:
    splits = jax.random.split(jax.random.key(seed), 5)
    load_gap = draw_load_gap(jax.random.fold_in(splits[4], 71), 0)
    profiles = jnp.clip(jnp.exp(math.log(0.3984375) - 2.9969585 * jax.random.uniform(splits[1], (USES, HOURS, SAMPLES), jnp.float32) ** block_scale(splits[1], (USES, HOURS, SAMPLES), ((1, 8), (2, 64)), -0.2, 0.2)), 0.019897461, 0.3984375).astype(jnp.bfloat16)
    slot_of_sample = draw_slot_of_sample(jax.random.fold_in(splits[4], 71), 0)
    slot_county = draw_slot_county(jax.random.fold_in(splits[4], 71), 0)
    return dict(load_gap=load_gap, profiles=profiles, slot_of_sample=slot_of_sample, slot_county=slot_county)


epsilon = 1e-06

def root_mean(values, count):
    return jnp.sqrt(jnp.sum(values * values) / count + epsilon)

def sample_counties(slot_of_sample, slot_county, device):
    slot_part = lax.dynamic_slice_in_dim(slot_of_sample, device * SAMP_DEV, SAMP_DEV, 0)
    row_values = lax.dynamic_index_in_dim(slot_county, device, 0, keepdims=False)
    return jnp.take(row_values, slot_part)

def apply_forward(profiles, slot_of_sample, slot_county, weights_in):

    def add_block(running, device):
        block_values = lax.dynamic_slice_in_dim(profiles, device * SAMP_DEV, SAMP_DEV, 2)
        weights_part = lax.dynamic_slice_in_dim(weights_in, device * SAMP_DEV, SAMP_DEV, 1)
        counties = sample_counties(slot_of_sample, slot_county, device)
        weighted = (block_values.astype(jnp.float32) * weights_part[:, None, :]).astype(jnp.bfloat16)
        columns = weighted.reshape(USES * HOURS, SAMP_DEV).T.astype(jnp.float32)
        return (running + jax.ops.segment_sum(columns, counties, num_segments=COUNTIES), None)
    running = jnp.zeros((COUNTIES, USES * HOURS), jnp.float32)
    running, _ = lax.scan(add_block, running, jnp.arange(N_SAMP, dtype=jnp.int32))
    return running.reshape(COUNTIES, USES, HOURS)

def apply_backward(profiles, slot_of_sample, slot_county, county_field):

    def one_block(carry, device):
        block_values = lax.dynamic_slice_in_dim(profiles, device * SAMP_DEV, SAMP_DEV, 2)
        counties = sample_counties(slot_of_sample, slot_county, device)
        row_values = jnp.take(county_field, counties, axis=0)
        pieces = lax.optimization_barrier(jnp.sum(block_values.astype(jnp.float32) * jnp.transpose(row_values, (1, 2, 0)), axis=1))
        return (carry, pieces)
    _, pieces = lax.scan(one_block, jnp.zeros((), jnp.float32), jnp.arange(N_SAMP, dtype=jnp.int32))
    return jnp.transpose(pieces, (1, 0, 2)).reshape(USES, SAMPLES)

def reference(load_gap, profiles, slot_of_sample, slot_county):
    space_count = COUNTIES * USES * HOURS
    sample_count = USES * SAMPLES
    beta_one = root_mean(load_gap, space_count)
    first_load = load_gap / beta_one
    image_one = apply_backward(profiles, slot_of_sample, slot_county, first_load)
    alpha_one = root_mean(image_one, sample_count)
    vector_one = image_one / alpha_one
    mismatch = apply_forward(profiles, slot_of_sample, slot_county, vector_one) - alpha_one * first_load
    beta_two = root_mean(mismatch, space_count)
    load_dir = mismatch / beta_two
    image_two = apply_backward(profiles, slot_of_sample, slot_county, load_dir) - beta_two * vector_one
    alpha_two = root_mean(image_two, sample_count)
    vector_two = image_two / alpha_two
    rho_value = jnp.sqrt(alpha_one * alpha_one + beta_two * beta_two)
    cosine = alpha_one / rho_value
    sine = beta_two / rho_value
    weight_step = cosine * beta_one / rho_value * vector_one
    search_dir = vector_two - sine * alpha_two / rho_value * vector_one
    return (weight_step, search_dir, load_dir)
```

```python
import jax
import jax.numpy as jnp
from jax import lax
from jax.sharding import PartitionSpec as P

epsilon = 1e-06
PAD = 48


def two_pieces(x, axis):
    high = lax.reduce_precision(x, 8, 7)
    return jnp.concatenate([high, x - high], axis=axis).astype(jnp.bfloat16)


def local(load_gap, profiles, slot_of_sample, slot_county):
    owners = lax.axis_size("samp")
    hour_count = lax.axis_size("hour")
    owner_index = lax.axis_index("samp")
    hour_index = lax.axis_index("hour")
    use_count, hour_dev, samp_dev = profiles.shape
    per_owner = load_gap.shape[0]
    row_width = use_count * hour_dev
    share_len = samp_dev // hour_count
    space_count = float(per_owner * owners * row_width * hour_count)
    sample_count = float(use_count * samp_dev * owners)
    my_counties = lax.dynamic_index_in_dim(slot_county, owner_index, 0, keepdims=False)
    county = jnp.take(my_counties, slot_of_sample)
    place = county // per_owner * PAD + county % per_owner
    places = jnp.arange(owners * PAD, dtype=jnp.int32)
    onehot = (places[:, None] == place[None, :]).astype(jnp.bfloat16)
    wide = profiles.astype(jnp.float32)

    def padded(rows):
        return jnp.pad(rows, ((0, PAD - per_owner), (0, 0)))

    def backward(rows):
        everyone = lax.all_gather(padded(rows), "samp", tiled=True)
        square = jnp.sum(everyone * everyone)
        pieces = two_pieces(everyone, 1)
        spread = lax.dot_general(
            pieces, onehot, (((0,), (0,)), ((), ())), preferred_element_type=jnp.float32
        )
        spread = (spread[:row_width] + spread[row_width:]).reshape(use_count, hour_dev, samp_dev)
        partial = jnp.sum(wide * spread, axis=1)
        extra = jnp.zeros((1, samp_dev), jnp.float32).at[0, 0].set(square)
        total = lax.psum(jnp.concatenate([partial, extra], axis=0), "hour")
        return total[:use_count], total[use_count, 0]

    def my_share(x):
        return lax.dynamic_slice_in_dim(x, hour_index * share_len, share_len, 1)

    gap_rows = load_gap.reshape(per_owner, row_width)
    plain, gap_total = backward(gap_rows)
    beta_one = jnp.sqrt(gap_total / space_count + epsilon)
    image = plain / beta_one
    weighted = (wide * image[:, None, :]).reshape(row_width, samp_dev)
    sums = lax.dot_general(
        onehot, two_pieces(weighted, 0), (((1,), (1,)), ((), ())), preferred_element_type=jnp.float32
    )
    sums = (sums[:, :row_width] + sums[:, row_width:]).reshape(owners, PAD, row_width)
    mine = jnp.sum(image * image)
    row = jnp.arange(PAD, dtype=jnp.int32)[None, :, None]
    sums = jnp.where(row == per_owner, mine, sums).reshape(owners * PAD, row_width)
    owned = lax.psum_scatter(sums, "samp", scatter_dimension=0, tiled=True)
    alpha_one = jnp.sqrt(owned[per_owner, 0] / sample_count + epsilon)
    mismatch = owned[:per_owner] / alpha_one - (alpha_one / beta_one) * gap_rows
    back, mismatch_total = backward(mismatch)
    beta_two = jnp.sqrt(mismatch_total / space_count + epsilon)
    load_dir = mismatch / beta_two
    vector_one = image / alpha_one
    image_two = back / beta_two - beta_two * vector_one
    second_total = lax.psum(jnp.sum(image_two * image_two), "samp")
    alpha_two = jnp.sqrt(second_total / sample_count + epsilon)
    rho_value = jnp.sqrt(alpha_one * alpha_one + beta_two * beta_two)
    cosine = alpha_one / rho_value
    sine = beta_two / rho_value
    vector_share = my_share(vector_one)
    weight_step = cosine * beta_one / rho_value * vector_share
    search_dir = my_share(image_two) / alpha_two - sine * alpha_two / rho_value * vector_share
    return (weight_step, search_dir, load_dir.reshape(per_owner, use_count, hour_dev))


def solution(mesh):
    return jax.shard_map(
        local,
        mesh=mesh,
        in_specs=(P("samp", None, "hour"), P(None, "hour", "samp"), P("samp"), P()),
        out_specs=(P(None, ("samp", "hour")), P(None, ("samp", "hour")), P("samp", None, "hour")),
        check_vma=False,
    )
```

```python
import jax
import jax.numpy as jnp
from jax import lax
from jax.experimental import pallas as pl
from jax.experimental.pallas import tpu as pltpu
from jax.sharding import PartitionSpec as P

epsilon = 1e-06
PAD = 48
MESH = pl.DeviceIdType.MESH
NY = 4
NZ = 16
UP = NZ // 2
DOWN = NZ - 1 - UP


def remote(src, dst, send_sem, recv_sem, **device):
    return pltpu.make_async_remote_copy(
        src_ref=src, dst_ref=dst, send_sem=send_sem, recv_sem=recv_sem,
        device_id=device, device_id_type=MESH,
    )


def at_place(z, y):
    return lax.rem(z + NZ, NZ) * NY + lax.rem(y + NY, NY)


def greet(axis, peers):
    barrier = pltpu.get_barrier_semaphore()
    for peer in peers:
        pl.semaphore_signal(barrier, inc=1, device_id={axis: peer}, device_id_type=MESH)
    return len(peers)


def near_peers(z, y):
    return [at_place(z, y + d) for d in range(1, NY)] + [at_place(z + 1, y), at_place(z - 1, y)]


def gather_body(in_ref, out_ref, send_y, recv_y, send_z, recv_z):
    me = lax.axis_index("samp")
    z, y = me // NY, lax.rem(me, NY)

    def y_copy(d):
        return remote(in_ref, out_ref.at[me], send_y.at[d], recv_y.at[d], samp=at_place(z, y + d))

    def y_arrival(d):
        slot = out_ref.at[at_place(z, y - d)]
        return remote(slot, slot, send_y.at[d], recv_y.at[d], samp=at_place(z, y + d))

    def z_copy(way, k, j, own=False):
        step = 1 - 2 * way
        slot = out_ref.at[at_place(z - step * k, y - j)]
        return remote(
            in_ref if own else slot, slot, send_z.at[way, k, j], recv_z.at[way, k, j],
            samp=at_place(z + step, y),
        )

    def z_arrival(way, k, j):
        step = 1 - 2 * way
        slot = out_ref.at[at_place(z - step * (k + 1), y - j)]
        return remote(slot, slot, send_z.at[way, k, j], recv_z.at[way, k, j], samp=at_place(z + step, y))

    z_copy(0, 0, 0, True).start()
    z_copy(1, 0, 0, True).start()
    for d in (2, 1, 3):
        y_copy(d).start()
    out_ref[pl.ds(me, 1)] = in_ref[...][None]
    for j in (1, 3, 2):
        y_arrival(j).wait_recv()
        z_copy(0, 0, j).start()
        z_copy(1, 0, j).start()

    def hop(k, carry):
        for j in (0, 1, 3, 2):
            for way in (0, 1):
                z_arrival(way, k - 1, j).wait_recv()
                z_copy(way, k, j).start()
        return carry

    lax.fori_loop(1, DOWN, hop, 0)
    for j in (0, 1, 3, 2):
        z_arrival(0, UP - 2, j).wait_recv()
        z_copy(0, UP - 1, j).start()
        z_arrival(1, DOWN - 1, j).wait_recv()
    for d in (2, 1, 3):
        y_copy(d).wait_send()
    z_copy(0, 0, 0, True).wait_send()
    z_copy(1, 0, 0, True).wait_send()
    for j in (1, 3, 2):
        z_copy(0, 0, j).wait_send()
        z_copy(1, 0, j).wait_send()

    def drain(k, carry):
        for j in (0, 1, 3, 2):
            for way in (0, 1):
                z_copy(way, k, j).wait_send()
        return carry

    lax.fori_loop(1, DOWN, drain, 0)
    for j in (0, 1, 3, 2):
        z_copy(0, UP - 1, j).wait_send()
        z_arrival(0, UP - 1, j).wait_recv()


def gather_kernel(in_ref, out_ref, got, send_y, recv_y, send_z, recv_z):
    me = lax.axis_index("samp")
    z, y = me // NY, lax.rem(me, NY)
    pl.semaphore_wait(pltpu.get_barrier_semaphore(), greet("samp", near_peers(z, y)))
    gather_body(in_ref, got, send_y, recv_y, send_z, recv_z)
    out_ref[...] = got[...]


def vmem(count):
    return [pl.BlockSpec(memory_space=pltpu.VMEM)] * count


def everyone_of(rows, number):
    count = NY * NZ
    dma = pltpu.SemaphoreType.DMA
    return pl.pallas_call(
        gather_kernel,
        out_shape=jax.ShapeDtypeStruct((count, *rows.shape), jnp.float32),
        in_specs=vmem(1),
        out_specs=vmem(1)[0],
        scratch_shapes=[
            pltpu.VMEM((count, *rows.shape), jnp.float32),
            dma((NY,)), dma((NY,)), dma((2, UP, NY)), dma((2, UP, NY)),
        ],
        compiler_params=pltpu.CompilerParams(collective_id=number, has_side_effects=True),
    )(rows).reshape(count * rows.shape[0], rows.shape[1])


def scatter_kernel(in_ref, out_ref, held, total, arrived, send_y, recv_y, send_z, recv_z):
    me = lax.axis_index("samp")
    z, y = me // NY, lax.rem(me, NY)
    order = (2, 1, 3, 0)

    def z_copy(way, k, j, own=False):
        step = 1 - 2 * way
        far = (UP, DOWN)[way] - k
        src = in_ref.at[at_place(z + step * far, y + j)] if own else held.at[way, k - 1, j]
        return remote(
            src, held.at[way, k, j], send_z.at[way, k, j], recv_z.at[way, k, j],
            samp=at_place(z + step, y),
        )

    def z_arrival(way, k, j):
        step = 1 - 2 * way
        slot = held.at[way, k, j]
        return remote(slot, slot, send_z.at[way, k, j], recv_z.at[way, k, j], samp=at_place(z + step, y))

    def add_own(way, k, j):
        step = 1 - 2 * way
        far = (UP, DOWN)[way] - k
        z_arrival(way, k - 1, j).wait_recv()
        held[way, k - 1, j] = held[way, k - 1, j] + in_ref[at_place(z + step * far, y + j)]
        z_copy(way, k, j).start()

    def y_copy(d):
        return remote(total.at[d], arrived.at[d], send_y.at[d], recv_y.at[d], samp=at_place(z, y + d))

    pl.semaphore_wait(pltpu.get_barrier_semaphore(), greet("samp", near_peers(z, y)))
    for j in order:
        for way in (0, 1):
            z_copy(way, 0, j, True).start()

    def hop(k, carry):
        for j in order:
            for way in (0, 1):
                add_own(way, k, j)
        return carry

    lax.fori_loop(1, DOWN, hop, 0)
    for j in order:
        add_own(0, UP - 1, j)
    for j in order:
        z_arrival(1, DOWN - 1, j).wait_recv()
        z_arrival(0, UP - 1, j).wait_recv()
        total[j] = held[0, UP - 1, j] + held[1, DOWN - 1, j] + in_ref[at_place(z, y + j)]
        if j:
            y_copy(j).start()

    def drain(k, carry):
        for j in order:
            for way in (0, 1):
                z_copy(way, k, j).wait_send()
        return carry

    for j in order:
        for way in (0, 1):
            z_copy(way, 0, j, True).wait_send()
    lax.fori_loop(1, DOWN, drain, 0)
    for j in order:
        z_copy(0, UP - 1, j).wait_send()
    for d in (1, 3, 2):
        y_copy(d).wait()
    out_ref[...] = total[0] + arrived[1] + arrived[2] + arrived[3]


def owned_of(sums, number):
    block = sums.shape[1:]
    dma = pltpu.SemaphoreType.DMA
    return pl.pallas_call(
        scatter_kernel,
        out_shape=jax.ShapeDtypeStruct(block, jnp.float32),
        in_specs=vmem(1),
        out_specs=vmem(1)[0],
        scratch_shapes=[
            pltpu.VMEM((2, UP, NY, *block), jnp.float32),
            pltpu.VMEM((NY, *block), jnp.float32),
            pltpu.VMEM((NY, *block), jnp.float32),
            dma((NY,)), dma((NY,)), dma((2, UP, NY)), dma((2, UP, NY)),
        ],
        compiler_params=pltpu.CompilerParams(collective_id=number, has_side_effects=True),
    )(sums)


def hour_kernel(n, in_ref, out_ref, arrived, send_sem, recv_sem):
    me = lax.axis_index("hour")
    order = [n // 2] + [d for d in range(1, n) if d != n // 2]

    def copy(d):
        return remote(in_ref, arrived.at[d], send_sem.at[d], recv_sem.at[d], hour=lax.rem(me + d, n))

    peers = [lax.rem(me + d, n) for d in order]
    pl.semaphore_wait(pltpu.get_barrier_semaphore(), greet("hour", peers))
    for d in order:
        copy(d).start()
    arrived[0] = in_ref[...]
    for d in order:
        copy(d).wait()
    out_ref[...] = jnp.sum(arrived[...], axis=0)


def hour_total(x, number):
    n = lax.axis_size("hour")
    dma = pltpu.SemaphoreType.DMA
    return pl.pallas_call(
        lambda *refs: hour_kernel(n, *refs),
        out_shape=jax.ShapeDtypeStruct(x.shape, jnp.float32),
        in_specs=vmem(1),
        out_specs=vmem(1)[0],
        scratch_shapes=[pltpu.VMEM((n, *x.shape), jnp.float32), dma((n,)), dma((n,))],
        compiler_params=pltpu.CompilerParams(collective_id=number, has_side_effects=True),
    )(x)


def samp_kernel(in_ref, out_ref, first, middle, second, send_y, recv_y, send_z, recv_z):
    me = lax.axis_index("samp")
    z, y = me // NY, lax.rem(me, NY)
    far_first = sorted(range(1, NZ), key=lambda d: -min(d, NZ - d))

    def y_copy(d):
        return remote(in_ref, first.at[d], send_y.at[d], recv_y.at[d], samp=at_place(z, y + d))

    def z_copy(d):
        return remote(middle, second.at[d], send_z.at[d], recv_z.at[d], samp=at_place(z + d, y))

    peers = [at_place(z + d, y) for d in far_first] + [at_place(z, y + d) for d in (2, 1, 3)]
    pl.semaphore_wait(pltpu.get_barrier_semaphore(), greet("samp", peers))
    for d in (2, 1, 3):
        y_copy(d).start()
    first[0] = in_ref[...]
    for d in (1, 3, 2):
        y_copy(d).wait()
    middle[...] = jnp.sum(first[...], axis=0)
    for d in far_first:
        z_copy(d).start()
    second[0] = middle[...]
    for d in far_first[::-1]:
        z_copy(d).wait()
    out_ref[...] = jnp.sum(second[...], axis=0)


def samp_total(x, number):
    dma = pltpu.SemaphoreType.DMA
    return pl.pallas_call(
        samp_kernel,
        out_shape=jax.ShapeDtypeStruct(x.shape, jnp.float32),
        in_specs=vmem(1),
        out_specs=vmem(1)[0],
        scratch_shapes=[
            pltpu.VMEM((NY, *x.shape), jnp.float32),
            pltpu.VMEM(x.shape, jnp.float32),
            pltpu.VMEM((NZ, *x.shape), jnp.float32),
            dma((NY,)), dma((NY,)), dma((NZ,)), dma((NZ,)),
        ],
        compiler_params=pltpu.CompilerParams(collective_id=number, has_side_effects=True),
    )(x)


def two_pieces(x, axis):
    high = lax.reduce_precision(x, 8, 7)
    return jnp.concatenate([high, x - high], axis=axis).astype(jnp.bfloat16)


def local(load_gap, profiles, slot_of_sample, slot_county):
    owners = lax.axis_size("samp")
    hour_count = lax.axis_size("hour")
    owner_index = lax.axis_index("samp")
    hour_index = lax.axis_index("hour")
    use_count, hour_dev, samp_dev = profiles.shape
    per_owner = load_gap.shape[0]
    row_width = use_count * hour_dev
    share_len = samp_dev // hour_count
    space_count = float(per_owner * owners * row_width * hour_count)
    sample_count = float(use_count * samp_dev * owners)
    my_counties = lax.dynamic_index_in_dim(slot_county, owner_index, 0, keepdims=False)
    county = jnp.take(my_counties, slot_of_sample)
    place = county // per_owner * PAD + county % per_owner
    places = jnp.arange(owners * PAD, dtype=jnp.int32)
    onehot = (places[:, None] == place[None, :]).astype(jnp.bfloat16)
    wide = profiles.astype(jnp.float32)

    def padded(rows):
        return jnp.pad(rows, ((0, PAD - per_owner), (0, 0)))

    def backward(rows, number):
        everyone = everyone_of(padded(rows), number)
        square = jnp.sum(everyone * everyone)
        pieces = two_pieces(everyone, 1)
        spread = lax.dot_general(
            pieces, onehot, (((0,), (0,)), ((), ())), preferred_element_type=jnp.float32
        )
        spread = (spread[:row_width] + spread[row_width:]).reshape(use_count, hour_dev, samp_dev)
        partial = jnp.sum(wide * spread, axis=1)
        rest = jnp.full((8, 128), square)
        total = hour_total(jnp.concatenate([partial.reshape(-1, 128), rest], axis=0), number + 1)
        return total[:-8].reshape(use_count, samp_dev), total[-1, 0]

    def my_share(x):
        return lax.dynamic_slice_in_dim(x, hour_index * share_len, share_len, 1)

    gap_rows = load_gap.reshape(per_owner, row_width)
    plain, gap_total = backward(gap_rows, 1)
    beta_one = jnp.sqrt(gap_total / space_count + epsilon)
    image = plain / beta_one
    weighted = (wide * image[:, None, :]).reshape(row_width, samp_dev)
    sums = lax.dot_general(
        onehot, two_pieces(weighted, 0), (((1,), (1,)), ((), ())), preferred_element_type=jnp.float32
    )
    sums = (sums[:, :row_width] + sums[:, row_width:]).reshape(owners, PAD, row_width)
    mine = jnp.sum(image * image)
    row = jnp.arange(PAD, dtype=jnp.int32)[None, :, None]
    sums = jnp.where(row == per_owner, mine, sums)
    owned = owned_of(sums, 5)
    alpha_one = jnp.sqrt(owned[per_owner, 0] / sample_count + epsilon)
    mismatch = owned[:per_owner] / alpha_one - (alpha_one / beta_one) * gap_rows
    back, mismatch_total = backward(mismatch, 3)
    beta_two = jnp.sqrt(mismatch_total / space_count + epsilon)
    load_dir = mismatch / beta_two
    vector_one = image / alpha_one
    image_two = back / beta_two - beta_two * vector_one
    second_total = samp_total(jnp.full((8, 128), jnp.sum(image_two * image_two)), 6)[0, 0]
    alpha_two = jnp.sqrt(second_total / sample_count + epsilon)
    rho_value = jnp.sqrt(alpha_one * alpha_one + beta_two * beta_two)
    cosine = alpha_one / rho_value
    sine = beta_two / rho_value
    vector_share = my_share(vector_one)
    weight_step = cosine * beta_one / rho_value * vector_share
    search_dir = my_share(image_two) / alpha_two - sine * alpha_two / rho_value * vector_share
    return (weight_step, search_dir, load_dir.reshape(per_owner, use_count, hour_dev))


def solution(mesh):
    return jax.shard_map(
        local,
        mesh=mesh,
        in_specs=(P("samp", None, "hour"), P(None, "hour", "samp"), P("samp"), P()),
        out_specs=(P(None, ("samp", "hour")), P(None, ("samp", "hour")), P("samp", None, "hour")),
        check_vma=False,
    )
```

```python
import jax
import jax.numpy as jnp
from jax import lax
from jax.experimental import pallas as pl
from jax.experimental.pallas import tpu as pltpu
from jax.sharding import PartitionSpec as P

epsilon = 1e-06
PAD = 48
HALF = 24
MESH = pl.DeviceIdType.MESH
NY = 4
NZ = 16
UP = NZ // 2
DOWN = NZ - 1 - UP


def remote(src, dst, send_sem, recv_sem, **device):
    return pltpu.make_async_remote_copy(
        src_ref=src, dst_ref=dst, send_sem=send_sem, recv_sem=recv_sem,
        device_id=device, device_id_type=MESH,
    )


def at_place(z, y):
    return lax.rem(z + NZ, NZ) * NY + lax.rem(y + NY, NY)


def greet(axis, peers):
    barrier = pltpu.get_barrier_semaphore()
    for peer in peers:
        pl.semaphore_signal(barrier, inc=1, device_id={axis: peer}, device_id_type=MESH)
    return len(peers)


def near_peers(z, y):
    return [at_place(z, y + d) for d in range(1, NY)] + [at_place(z + 1, y), at_place(z - 1, y)]


def gather_body(in_ref, out_ref, send_y, recv_y, send_z, recv_z, send_t, recv_t, send_u, recv_u):
    me = lax.axis_index("samp")
    z, y = me // NY, lax.rem(me, NY)
    top, bottom = pl.ds(0, HALF), pl.ds(HALF, PAD - HALF)

    def y_copy(d):
        return remote(
            in_ref.at[top], out_ref.at[me, top], send_y.at[d], recv_y.at[d], samp=at_place(z, y + d)
        )

    def y_arrival(d):
        slot = out_ref.at[at_place(z, y - d), top]
        return remote(slot, slot, send_y.at[d], recv_y.at[d], samp=at_place(z, y + d))

    def z_copy(way, k, j, own=False):
        step = 1 - 2 * way
        slot = out_ref.at[at_place(z - step * k, y - j), top]
        return remote(
            in_ref.at[top] if own else slot, slot, send_z.at[way, k, j], recv_z.at[way, k, j],
            samp=at_place(z + step, y),
        )

    def z_arrival(way, k, j):
        step = 1 - 2 * way
        slot = out_ref.at[at_place(z - step * (k + 1), y - j), top]
        return remote(slot, slot, send_z.at[way, k, j], recv_z.at[way, k, j], samp=at_place(z + step, y))

    def t_copy(way, k, own=False):
        step = 1 - 2 * way
        slot = out_ref.at[at_place(z - step * k, y), bottom]
        return remote(
            in_ref.at[bottom] if own else slot, slot, send_t.at[way, k], recv_t.at[way, k],
            samp=at_place(z + step, y),
        )

    def t_arrival(way, k):
        step = 1 - 2 * way
        slot = out_ref.at[at_place(z - step * (k + 1), y), bottom]
        return remote(slot, slot, send_t.at[way, k], recv_t.at[way, k], samp=at_place(z + step, y))

    def u_copy(off, d, own=False):
        slot = out_ref.at[at_place(z + off, y), bottom]
        return remote(
            in_ref.at[bottom] if own else slot, slot, send_u.at[off, d], recv_u.at[off, d],
            samp=at_place(z, y + d),
        )

    def u_arrival(off, d):
        slot = out_ref.at[at_place(z + off, y - d), bottom]
        return remote(slot, slot, send_u.at[off, d], recv_u.at[off, d], samp=at_place(z, y + d))

    for way in (0, 1):
        t_copy(way, 0, True).start()
        z_copy(way, 0, 0, True).start()
    for d in (2, 1, 3):
        y_copy(d).start()
    for d in (2, 1, 3):
        u_copy(0, d, True).start()
    out_ref[pl.ds(me, 1)] = in_ref[...][None]
    for j in (1, 3, 2):
        y_arrival(j).wait_recv()
        for way in (0, 1):
            z_copy(way, 0, j).start()

    def fan_out(way, k):
        off = NZ - 1 - k if way == 0 else k + 1
        for d in (2, 1, 3):
            u_copy(off, d).start()

    def hop(k, carry):
        for way in (0, 1):
            t_arrival(way, k - 1).wait_recv()
            t_copy(way, k).start()
            fan_out(way, k - 1)
        for j in (0, 1, 3, 2):
            for way in (0, 1):
                z_arrival(way, k - 1, j).wait_recv()
                z_copy(way, k, j).start()
        return carry

    lax.fori_loop(1, DOWN, hop, 0)
    t_arrival(0, UP - 2).wait_recv()
    t_copy(0, UP - 1).start()
    fan_out(0, UP - 2)
    t_arrival(1, DOWN - 1).wait_recv()
    fan_out(1, DOWN - 1)
    for j in (0, 1, 3, 2):
        z_arrival(0, UP - 2, j).wait_recv()
        z_copy(0, UP - 1, j).start()
        z_arrival(1, DOWN - 1, j).wait_recv()
    t_arrival(0, UP - 1).wait_recv()
    fan_out(0, UP - 1)
    for d in (2, 1, 3):
        y_copy(d).wait_send()
        u_copy(0, d, True).wait_send()
        u_arrival(0, d).wait_recv()
    for way in (0, 1):
        t_copy(way, 0, True).wait_send()
        z_copy(way, 0, 0, True).wait_send()
        for j in (1, 3, 2):
            z_copy(way, 0, j).wait_send()

    def drain(k, carry):
        for way in (0, 1):
            t_copy(way, k).wait_send()
            for j in (0, 1, 3, 2):
                z_copy(way, k, j).wait_send()
        return carry

    lax.fori_loop(1, DOWN, drain, 0)

    def drain_u(off, carry):
        for d in (2, 1, 3):
            u_copy(off, d).wait_send()
            u_arrival(off, d).wait_recv()
        return carry

    lax.fori_loop(1, NZ, drain_u, 0)
    t_copy(0, UP - 1).wait_send()
    for j in (0, 1, 3, 2):
        z_copy(0, UP - 1, j).wait_send()
        z_arrival(0, UP - 1, j).wait_recv()


def gather_kernel(in_ref, out_ref, got, *sems):
    me = lax.axis_index("samp")
    z, y = me // NY, lax.rem(me, NY)
    pl.semaphore_wait(pltpu.get_barrier_semaphore(), greet("samp", near_peers(z, y)))
    gather_body(in_ref, got, *sems)
    out_ref[...] = got[...]


def vmem(count):
    return [pl.BlockSpec(memory_space=pltpu.VMEM)] * count


def everyone_of(rows, number):
    count = NY * NZ
    dma = pltpu.SemaphoreType.DMA
    return pl.pallas_call(
        gather_kernel,
        out_shape=jax.ShapeDtypeStruct((count, *rows.shape), jnp.float32),
        in_specs=vmem(1),
        out_specs=vmem(1)[0],
        scratch_shapes=[
            pltpu.VMEM((count, *rows.shape), jnp.float32),
            dma((NY,)), dma((NY,)), dma((2, UP, NY)), dma((2, UP, NY)),
            dma((2, UP)), dma((2, UP)), dma((NZ, NY)), dma((NZ, NY)),
        ],
        compiler_params=pltpu.CompilerParams(collective_id=number, has_side_effects=True),
    )(rows).reshape(count * rows.shape[0], rows.shape[1])


def scatter_body(
    in_ref, out_ref, held, total, arrived, crossed, chain, first,
    send_y, recv_y, send_z, recv_z, send_t, recv_t, send_u, recv_u,
):
    me = lax.axis_index("samp")
    z, y = me // NY, lax.rem(me, NY)
    top, bottom = pl.ds(0, HALF), pl.ds(HALF, PAD - HALF)
    order = (2, 1, 3, 0)

    def target(way, k):
        return (UP - k) if way == 0 else (NZ - DOWN + k)

    def z_copy(way, k, j, own=False):
        src = in_ref.at[at_place(z + target(way, k), y + j), top] if own else held.at[way, k - 1, j]
        return remote(
            src, held.at[way, k, j], send_z.at[way, k, j], recv_z.at[way, k, j],
            samp=at_place(z + 1 - 2 * way, y),
        )

    def z_arrival(way, k, j):
        slot = held.at[way, k, j]
        return remote(
            slot, slot, send_z.at[way, k, j], recv_z.at[way, k, j], samp=at_place(z + 1 - 2 * way, y)
        )

    def add_own(way, k, j):
        z_arrival(way, k - 1, j).wait_recv()
        held[way, k - 1, j] = held[way, k - 1, j] + in_ref[at_place(z + target(way, k), y + j), top]
        z_copy(way, k, j).start()

    def u_copy(off, d):
        return remote(
            in_ref.at[at_place(z + off, y + d), bottom], crossed.at[off, d],
            send_u.at[off, d], recv_u.at[off, d], samp=at_place(z, y + d),
        )

    def crossed_sum(off):
        for d in (1, 3, 2):
            u_copy(off, d).wait_recv()
        own = in_ref[at_place(z + off, y), bottom]
        return own + crossed[off, 1] + crossed[off, 2] + crossed[off, 3]

    def t_copy(way, k, own=False):
        return remote(
            first.at[way] if own else chain.at[way, k - 1], chain.at[way, k],
            send_t.at[way, k], recv_t.at[way, k], samp=at_place(z + 1 - 2 * way, y),
        )

    def t_arrival(way, k):
        slot = chain.at[way, k]
        return remote(slot, slot, send_t.at[way, k], recv_t.at[way, k], samp=at_place(z + 1 - 2 * way, y))

    def add_crossed(way, k):
        mine = crossed_sum(target(way, k))
        t_arrival(way, k - 1).wait_recv()
        chain[way, k - 1] = chain[way, k - 1] + mine
        t_copy(way, k).start()

    def y_copy(d):
        return remote(total.at[d], arrived.at[d], send_y.at[d], recv_y.at[d], samp=at_place(z, y + d))

    def launch(k, carry):
        for way in (0, 1):
            for d in (2, 1, 3):
                u_copy(target(way, k), d).start()
        return carry

    launch(0, 0)
    for j in order:
        for way in (0, 1):
            z_copy(way, 0, j, True).start()
    lax.fori_loop(1, DOWN, launch, 0)
    for off in (1, 0):
        for d in (2, 1, 3):
            u_copy(off, d).start()
    for way in (0, 1):
        first[way] = crossed_sum(target(way, 0))
        t_copy(way, 0, True).start()

    def hop(k, carry):
        for j in order:
            for way in (0, 1):
                add_own(way, k, j)
        for way in (0, 1):
            add_crossed(way, k)
        return carry

    lax.fori_loop(1, DOWN, hop, 0)
    for j in order:
        add_own(0, UP - 1, j)
    add_crossed(0, UP - 1)
    for j in order:
        z_arrival(1, DOWN - 1, j).wait_recv()
        z_arrival(0, UP - 1, j).wait_recv()
        total[j] = held[0, UP - 1, j] + held[1, DOWN - 1, j] + in_ref[at_place(z, y + j), top]
        if j:
            y_copy(j).start()
    mine = crossed_sum(0)
    t_arrival(1, DOWN - 1).wait_recv()
    t_arrival(0, UP - 1).wait_recv()
    out_ref[bottom] = mine + chain[0, UP - 1] + chain[1, DOWN - 1]

    def drain(k, carry):
        for way in (0, 1):
            t_copy(way, k).wait_send()
            for j in order:
                z_copy(way, k, j).wait_send()
        return carry

    def drain_u(off, carry):
        for d in (2, 1, 3):
            u_copy(off, d).wait_send()
        return carry

    for way in (0, 1):
        t_copy(way, 0, True).wait_send()
        for j in order:
            z_copy(way, 0, j, True).wait_send()
    lax.fori_loop(1, DOWN, drain, 0)
    lax.fori_loop(0, NZ, drain_u, 0)
    t_copy(0, UP - 1).wait_send()
    for j in order:
        z_copy(0, UP - 1, j).wait_send()
    for d in (1, 3, 2):
        y_copy(d).wait()
    out_ref[top] = total[0] + arrived[1] + arrived[2] + arrived[3]


def scatter_kernel(in_ref, out_ref, *scratch):
    me = lax.axis_index("samp")
    z, y = me // NY, lax.rem(me, NY)
    pl.semaphore_wait(pltpu.get_barrier_semaphore(), greet("samp", near_peers(z, y)))
    scatter_body(in_ref, out_ref, *scratch)


def owned_of(sums, number):
    block = sums.shape[1:]
    upper, lower = (HALF, block[1]), (PAD - HALF, block[1])
    dma = pltpu.SemaphoreType.DMA
    return pl.pallas_call(
        scatter_kernel,
        out_shape=jax.ShapeDtypeStruct(block, jnp.float32),
        in_specs=vmem(1),
        out_specs=vmem(1)[0],
        scratch_shapes=[
            pltpu.VMEM((2, UP, NY, *upper), jnp.float32),
            pltpu.VMEM((NY, *upper), jnp.float32),
            pltpu.VMEM((NY, *upper), jnp.float32),
            pltpu.VMEM((NZ, NY, *lower), jnp.float32),
            pltpu.VMEM((2, UP, *lower), jnp.float32),
            pltpu.VMEM((2, *lower), jnp.float32),
            dma((NY,)), dma((NY,)), dma((2, UP, NY)), dma((2, UP, NY)),
            dma((2, UP)), dma((2, UP)), dma((NZ, NY)), dma((NZ, NY)),
        ],
        compiler_params=pltpu.CompilerParams(collective_id=number, has_side_effects=True),
    )(sums)


def hour_kernel(n, in_ref, out_ref, arrived, send_sem, recv_sem):
    me = lax.axis_index("hour")
    order = [n // 2] + [d for d in range(1, n) if d != n // 2]

    def copy(d):
        return remote(in_ref, arrived.at[d], send_sem.at[d], recv_sem.at[d], hour=lax.rem(me + d, n))

    peers = [lax.rem(me + d, n) for d in order]
    pl.semaphore_wait(pltpu.get_barrier_semaphore(), greet("hour", peers))
    for d in order:
        copy(d).start()
    arrived[0] = in_ref[...]
    for d in order:
        copy(d).wait()
    out_ref[...] = jnp.sum(arrived[...], axis=0)


def hour_total(x, number):
    n = lax.axis_size("hour")
    dma = pltpu.SemaphoreType.DMA
    return pl.pallas_call(
        lambda *refs: hour_kernel(n, *refs),
        out_shape=jax.ShapeDtypeStruct(x.shape, jnp.float32),
        in_specs=vmem(1),
        out_specs=vmem(1)[0],
        scratch_shapes=[pltpu.VMEM((n, *x.shape), jnp.float32), dma((n,)), dma((n,))],
        compiler_params=pltpu.CompilerParams(collective_id=number, has_side_effects=True),
    )(x)


def samp_kernel(in_ref, out_ref, first, middle, second, send_y, recv_y, send_z, recv_z):
    me = lax.axis_index("samp")
    z, y = me // NY, lax.rem(me, NY)
    far_first = sorted(range(1, NZ), key=lambda d: -min(d, NZ - d))

    def y_copy(d):
        return remote(in_ref, first.at[d], send_y.at[d], recv_y.at[d], samp=at_place(z, y + d))

    def z_copy(d):
        return remote(middle, second.at[d], send_z.at[d], recv_z.at[d], samp=at_place(z + d, y))

    peers = [at_place(z + d, y) for d in far_first] + [at_place(z, y + d) for d in (2, 1, 3)]
    pl.semaphore_wait(pltpu.get_barrier_semaphore(), greet("samp", peers))
    for d in (2, 1, 3):
        y_copy(d).start()
    first[0] = in_ref[...]
    for d in (1, 3, 2):
        y_copy(d).wait()
    middle[...] = jnp.sum(first[...], axis=0)
    for d in far_first:
        z_copy(d).start()
    second[0] = middle[...]
    for d in far_first[::-1]:
        z_copy(d).wait()
    out_ref[...] = jnp.sum(second[...], axis=0)


def samp_total(x, number):
    dma = pltpu.SemaphoreType.DMA
    return pl.pallas_call(
        samp_kernel,
        out_shape=jax.ShapeDtypeStruct(x.shape, jnp.float32),
        in_specs=vmem(1),
        out_specs=vmem(1)[0],
        scratch_shapes=[
            pltpu.VMEM((NY, *x.shape), jnp.float32),
            pltpu.VMEM(x.shape, jnp.float32),
            pltpu.VMEM((NZ, *x.shape), jnp.float32),
            dma((NY,)), dma((NY,)), dma((NZ,)), dma((NZ,)),
        ],
        compiler_params=pltpu.CompilerParams(collective_id=number, has_side_effects=True),
    )(x)


def two_pieces(x, axis):
    high = lax.reduce_precision(x, 8, 7)
    return jnp.concatenate([high, x - high], axis=axis).astype(jnp.bfloat16)


def local(load_gap, profiles, slot_of_sample, slot_county):
    owners = lax.axis_size("samp")
    hour_count = lax.axis_size("hour")
    owner_index = lax.axis_index("samp")
    hour_index = lax.axis_index("hour")
    use_count, hour_dev, samp_dev = profiles.shape
    per_owner = load_gap.shape[0]
    row_width = use_count * hour_dev
    share_len = samp_dev // hour_count
    space_count = float(per_owner * owners * row_width * hour_count)
    sample_count = float(use_count * samp_dev * owners)
    my_counties = lax.dynamic_index_in_dim(slot_county, owner_index, 0, keepdims=False)
    slots = jnp.arange(slot_county.shape[1], dtype=jnp.int32)
    county = jnp.sum(
        jnp.where(slots[:, None] == slot_of_sample[None, :], my_counties[:, None], 0), axis=0
    )
    place = county // per_owner * PAD + county % per_owner
    places = jnp.arange(owners * PAD, dtype=jnp.int32)
    onehot = (places[:, None] == place[None, :]).astype(jnp.bfloat16)
    wide = profiles.astype(jnp.float32)

    def padded(rows):
        return jnp.pad(rows, ((0, PAD - per_owner), (0, 0)))

    def backward(rows, number):
        everyone = everyone_of(padded(rows), number)
        square = jnp.sum(everyone * everyone)
        pieces = two_pieces(everyone, 1)
        spread = lax.dot_general(
            pieces, onehot, (((0,), (0,)), ((), ())), preferred_element_type=jnp.float32
        )
        spread = (spread[:row_width] + spread[row_width:]).reshape(use_count, hour_dev, samp_dev)
        partial = jnp.sum(wide * spread, axis=1)
        rest = jnp.full((8, 128), square)
        total = hour_total(jnp.concatenate([partial.reshape(-1, 128), rest], axis=0), number + 1)
        return total[:-8].reshape(use_count, samp_dev), total[-1, 0]

    def my_share(x):
        return lax.dynamic_slice_in_dim(x, hour_index * share_len, share_len, 1)

    gap_rows = load_gap.reshape(per_owner, row_width)
    plain, gap_total = backward(gap_rows, 1)
    beta_one = jnp.sqrt(gap_total / space_count + epsilon)
    image = plain / beta_one
    weighted = (wide * image[:, None, :]).reshape(row_width, samp_dev)
    sums = lax.dot_general(
        onehot, two_pieces(weighted, 0), (((1,), (1,)), ((), ())), preferred_element_type=jnp.float32
    )
    sums = (sums[:, :row_width] + sums[:, row_width:]).reshape(owners, PAD, row_width)
    mine = jnp.sum(image * image)
    row = jnp.arange(PAD, dtype=jnp.int32)[None, :, None]
    sums = jnp.where(row == per_owner, mine, sums)
    owned = owned_of(sums, 5)
    alpha_one = jnp.sqrt(owned[per_owner, 0] / sample_count + epsilon)
    mismatch = owned[:per_owner] / alpha_one - (alpha_one / beta_one) * gap_rows
    back, mismatch_total = backward(mismatch, 3)
    beta_two = jnp.sqrt(mismatch_total / space_count + epsilon)
    load_dir = mismatch / beta_two
    vector_one = image / alpha_one
    image_two = back / beta_two - beta_two * vector_one
    second_total = samp_total(jnp.full((8, 128), jnp.sum(image_two * image_two)), 6)[0, 0]
    alpha_two = jnp.sqrt(second_total / sample_count + epsilon)
    rho_value = jnp.sqrt(alpha_one * alpha_one + beta_two * beta_two)
    cosine = alpha_one / rho_value
    sine = beta_two / rho_value
    vector_share = my_share(vector_one)
    weight_step = cosine * beta_one / rho_value * vector_share
    search_dir = my_share(image_two) / alpha_two - sine * alpha_two / rho_value * vector_share
    return (weight_step, search_dir, load_dir.reshape(per_owner, use_count, hour_dev))


def solution(mesh):
    return jax.shard_map(
        local,
        mesh=mesh,
        in_specs=(P("samp", None, "hour"), P(None, "hour", "samp"), P("samp"), P()),
        out_specs=(P(None, ("samp", "hour")), P(None, ("samp", "hour")), P("samp", None, "hour")),
        check_vma=False,
    )
```

```python
import jax
import jax.numpy as jnp
from jax import lax
from jax.experimental import pallas as pl
from jax.experimental.pallas import tpu as pltpu
from jax.sharding import PartitionSpec as P

epsilon = 1e-06
PAD = 48
HALF = 24
GROUPS = 4
MESH = pl.DeviceIdType.MESH
NY = 4
NZ = 16
UP = NZ // 2
DOWN = NZ - 1 - UP


def remote(src, dst, send_sem, recv_sem, **device):
    return pltpu.make_async_remote_copy(
        src_ref=src, dst_ref=dst, send_sem=send_sem, recv_sem=recv_sem,
        device_id=device, device_id_type=MESH,
    )


def at_place(z, y):
    return lax.rem(z + NZ, NZ) * NY + lax.rem(y + NY, NY)


def greet(axis, peers):
    barrier = pltpu.get_barrier_semaphore()
    for peer in peers:
        pl.semaphore_signal(barrier, inc=1, device_id={axis: peer}, device_id_type=MESH)
    return len(peers)


def near_peers(z, y):
    return [at_place(z, y + d) for d in range(1, NY)] + [at_place(z + 1, y), at_place(z - 1, y)]


def gather_body(in_ref, out_ref, send_y, recv_y, send_z, recv_z, send_t, recv_t, send_u, recv_u):
    me = lax.axis_index("samp")
    z, y = me // NY, lax.rem(me, NY)
    side = NY * NZ

    def y_copy(d):
        return remote(
            in_ref.at[pl.ds(0, 1)], out_ref.at[pl.ds(NY - d, 1)], send_y.at[d], recv_y.at[d],
            samp=at_place(z, y + d),
        )

    def places(way, k):
        return ((NZ - k) % NZ, NZ - k - 1) if way == 0 else (k, k + 1)

    def z_copy(way, k):
        here, there = places(way, k)
        return remote(
            out_ref.at[pl.ds(NY * here, NY)], out_ref.at[pl.ds(NY * there, NY)],
            send_z.at[way, k], recv_z.at[way, k], samp=at_place(z + 1 - 2 * way, y),
        )

    def t_copy(way, k):
        here, there = places(way, k)
        src = in_ref.at[pl.ds(1, 1)] if k == 0 else out_ref.at[pl.ds(side + here, 1)]
        return remote(
            src, out_ref.at[pl.ds(side + there, 1)],
            send_t.at[way, k], recv_t.at[way, k], samp=at_place(z + 1 - 2 * way, y),
        )

    def u_copy(group, d):
        size = NZ // GROUPS
        return remote(
            out_ref.at[pl.ds(side + group * size, size)],
            out_ref.at[pl.ds(side + (NY - d) * NZ + group * size, size)],
            send_u.at[group, d], recv_u.at[group, d], samp=at_place(z, y + d),
        )

    steps = [(way, k) for k in range(UP) for way in (0, 1) if k < (UP, DOWN)[way]]
    for way in (0, 1):
        t_copy(way, 0).start()
    for d in (2, 1, 3):
        y_copy(d).start()
    out_ref[pl.ds(0, 1)] = in_ref[pl.ds(0, 1)]
    out_ref[pl.ds(side, 1)] = in_ref[pl.ds(1, 1)]
    for d in (1, 3, 2):
        y_copy(d).wait_recv()
    for way in (0, 1):
        z_copy(way, 0).start()
    landed = {0}
    sent = set()
    for way, k in steps:
        t_copy(way, k).wait_recv()
        landed.add(places(way, k)[1])
        if (way, k + 1) in steps:
            t_copy(way, k + 1).start()
        for group in range(GROUPS):
            size = NZ // GROUPS
            if group not in sent and landed.issuperset(range(group * size, group * size + size)):
                sent.add(group)
                for d in (2, 1, 3):
                    u_copy(group, d).start()
        z_copy(way, k).wait_recv()
        if (way, k + 1) in steps:
            z_copy(way, k + 1).start()
    for d in (2, 1, 3):
        y_copy(d).wait_send()
    for way, k in steps:
        t_copy(way, k).wait_send()
        z_copy(way, k).wait_send()
    for group in range(GROUPS):
        for d in (2, 1, 3):
            u_copy(group, d).wait()


def gather_kernel(in_ref, out_ref, got, *sems):
    me = lax.axis_index("samp")
    z, y = me // NY, lax.rem(me, NY)
    pl.semaphore_wait(pltpu.get_barrier_semaphore(), greet("samp", near_peers(z, y)))
    gather_body(in_ref, got, *sems)
    out_ref[...] = got[...]


def vmem(count):
    return [pl.BlockSpec(memory_space=pltpu.VMEM)] * count


def everyone_of(rows, number):
    whole = (2 * NY * NZ, HALF, rows.shape[1])
    dma = pltpu.SemaphoreType.DMA
    return pl.pallas_call(
        gather_kernel,
        out_shape=jax.ShapeDtypeStruct(whole, jnp.float32),
        in_specs=vmem(1),
        out_specs=vmem(1)[0],
        scratch_shapes=[
            pltpu.VMEM(whole, jnp.float32),
            dma((NY,)), dma((NY,)), dma((2, UP)), dma((2, UP)),
            dma((2, UP)), dma((2, UP)), dma((GROUPS, NY)), dma((GROUPS, NY)),
        ],
        compiler_params=pltpu.CompilerParams(collective_id=number, has_side_effects=True),
    )(rows.reshape(2, HALF, -1)).reshape(-1, rows.shape[1])


SPANS = ((6, 6), (2, 4), (12, 4), (0, 2))


def scatter_body(
    in_ref, out_ref, held, total, arrived, crossed, chain, first,
    send_y, recv_y, send_z, recv_z, send_t, recv_t, send_u, recv_u,
):
    me = lax.axis_index("samp")
    z, y = me // NY, lax.rem(me, NY)
    side = NY * NZ
    steps = [(way, k) for k in range(UP) for way in (0, 1) if k < (UP, DOWN)[way]]

    def target(way, k):
        return (UP - k) if way == 0 else (NZ - DOWN + k)

    def z_copy(way, k):
        src = in_ref.at[pl.ds(NY * target(way, k), NY)] if k == 0 else held.at[way, k - 1]
        return remote(
            src, held.at[way, k], send_z.at[way, k], recv_z.at[way, k],
            samp=at_place(z + 1 - 2 * way, y),
        )

    def u_copy(span, d):
        start, size = SPANS[span]
        return remote(
            in_ref.at[pl.ds(side + d * NZ + start, size)], crossed.at[d, pl.ds(start, size)],
            send_u.at[span, d], recv_u.at[span, d], samp=at_place(z, y + d),
        )

    def t_copy(way, k):
        return remote(
            first.at[way] if k == 0 else chain.at[way, k - 1], chain.at[way, k],
            send_t.at[way, k], recv_t.at[way, k], samp=at_place(z + 1 - 2 * way, y),
        )

    def y_copy(d):
        return remote(total.at[d], arrived.at[d], send_y.at[d], recv_y.at[d], samp=at_place(z, y + d))

    ready = set()

    def crossed_sum(off):
        for span, (start, size) in enumerate(SPANS):
            if start <= off < start + size and span not in ready:
                ready.add(span)
                for d in (1, 3, 2):
                    u_copy(span, d).wait_recv()
        return in_ref[side + off] + crossed[1, off] + crossed[2, off] + crossed[3, off]

    for span in range(len(SPANS)):
        for d in (2, 1, 3):
            u_copy(span, d).start()
        if span == 0:
            for way in (0, 1):
                z_copy(way, 0).start()
    for way in (0, 1):
        first[way] = crossed_sum(target(way, 0))
        t_copy(way, 0).start()
    for way, k in steps:
        if (way, k + 1) in steps:
            z_copy(way, k).wait_recv()
            held[way, k] = held[way, k] + in_ref[pl.ds(NY * target(way, k + 1), NY)]
            z_copy(way, k + 1).start()
            mine = crossed_sum(target(way, k + 1))
            t_copy(way, k).wait_recv()
            chain[way, k] = chain[way, k] + mine
            t_copy(way, k + 1).start()
    z_copy(1, DOWN - 1).wait_recv()
    z_copy(0, UP - 1).wait_recv()
    total[...] = held[0, UP - 1] + held[1, DOWN - 1] + in_ref[pl.ds(0, NY)]
    for d in (2, 1, 3):
        y_copy(d).start()
    mine = crossed_sum(0)
    t_copy(1, DOWN - 1).wait_recv()
    t_copy(0, UP - 1).wait_recv()
    out_ref[pl.ds(HALF, HALF)] = mine + chain[0, UP - 1] + chain[1, DOWN - 1]
    for way, k in steps:
        t_copy(way, k).wait_send()
        z_copy(way, k).wait_send()
    for span in range(len(SPANS)):
        for d in (2, 1, 3):
            u_copy(span, d).wait_send()
    for d in (1, 3, 2):
        y_copy(d).wait()
    out_ref[pl.ds(0, HALF)] = total[0] + arrived[1] + arrived[2] + arrived[3]


def scatter_kernel(in_ref, out_ref, *scratch):
    me = lax.axis_index("samp")
    z, y = me // NY, lax.rem(me, NY)
    pl.semaphore_wait(pltpu.get_barrier_semaphore(), greet("samp", near_peers(z, y)))
    scatter_body(in_ref, out_ref, *scratch)


def owned_of(sums, number):
    block = sums.shape[1:]
    dma = pltpu.SemaphoreType.DMA
    return pl.pallas_call(
        scatter_kernel,
        out_shape=jax.ShapeDtypeStruct((2 * block[0], block[1]), jnp.float32),
        in_specs=vmem(1),
        out_specs=vmem(1)[0],
        scratch_shapes=[
            pltpu.VMEM((2, UP, NY, *block), jnp.float32),
            pltpu.VMEM((NY, *block), jnp.float32),
            pltpu.VMEM((NY, *block), jnp.float32),
            pltpu.VMEM((NY, NZ, *block), jnp.float32),
            pltpu.VMEM((2, UP, *block), jnp.float32),
            pltpu.VMEM((2, *block), jnp.float32),
            dma((NY,)), dma((NY,)), dma((2, UP)), dma((2, UP)),
            dma((2, UP)), dma((2, UP)), dma((len(SPANS), NY)), dma((len(SPANS), NY)),
        ],
        compiler_params=pltpu.CompilerParams(collective_id=number, has_side_effects=True),
    )(sums)


def hour_kernel(n, in_ref, out_ref, arrived, send_sem, recv_sem):
    me = lax.axis_index("hour")
    order = [n // 2] + [d for d in range(1, n) if d != n // 2]

    def copy(d):
        return remote(in_ref, arrived.at[d], send_sem.at[d], recv_sem.at[d], hour=lax.rem(me + d, n))

    peers = [lax.rem(me + d, n) for d in order]
    pl.semaphore_wait(pltpu.get_barrier_semaphore(), greet("hour", peers))
    for d in order:
        copy(d).start()
    arrived[0] = in_ref[...]
    for d in order:
        copy(d).wait()
    out_ref[...] = jnp.sum(arrived[...], axis=0)


def hour_total(x, number):
    n = lax.axis_size("hour")
    dma = pltpu.SemaphoreType.DMA
    return pl.pallas_call(
        lambda *refs: hour_kernel(n, *refs),
        out_shape=jax.ShapeDtypeStruct(x.shape, jnp.float32),
        in_specs=vmem(1),
        out_specs=vmem(1)[0],
        scratch_shapes=[pltpu.VMEM((n, *x.shape), jnp.float32), dma((n,)), dma((n,))],
        compiler_params=pltpu.CompilerParams(collective_id=number, has_side_effects=True),
    )(x)


def samp_kernel(in_ref, out_ref, first, middle, second, send_y, recv_y, send_z, recv_z):
    me = lax.axis_index("samp")
    z, y = me // NY, lax.rem(me, NY)
    far_first = sorted(range(1, NZ), key=lambda d: -min(d, NZ - d))

    def y_copy(d):
        return remote(in_ref, first.at[d], send_y.at[d], recv_y.at[d], samp=at_place(z, y + d))

    def z_copy(d):
        return remote(middle, second.at[d], send_z.at[d], recv_z.at[d], samp=at_place(z + d, y))

    peers = [at_place(z + d, y) for d in far_first] + [at_place(z, y + d) for d in (2, 1, 3)]
    pl.semaphore_wait(pltpu.get_barrier_semaphore(), greet("samp", peers))
    for d in (2, 1, 3):
        y_copy(d).start()
    first[0] = in_ref[...]
    for d in (1, 3, 2):
        y_copy(d).wait()
    middle[...] = jnp.sum(first[...], axis=0)
    for d in far_first:
        z_copy(d).start()
    second[0] = middle[...]
    for d in far_first[::-1]:
        z_copy(d).wait()
    out_ref[...] = jnp.sum(second[...], axis=0)


def samp_total(x, number):
    dma = pltpu.SemaphoreType.DMA
    return pl.pallas_call(
        samp_kernel,
        out_shape=jax.ShapeDtypeStruct(x.shape, jnp.float32),
        in_specs=vmem(1),
        out_specs=vmem(1)[0],
        scratch_shapes=[
            pltpu.VMEM((NY, *x.shape), jnp.float32),
            pltpu.VMEM(x.shape, jnp.float32),
            pltpu.VMEM((NZ, *x.shape), jnp.float32),
            dma((NY,)), dma((NY,)), dma((NZ,)), dma((NZ,)),
        ],
        compiler_params=pltpu.CompilerParams(collective_id=number, has_side_effects=True),
    )(x)


def two_pieces(x, axis):
    high = lax.reduce_precision(x, 8, 7)
    return jnp.concatenate([high, x - high], axis=axis).astype(jnp.bfloat16)


def local(load_gap, profiles, slot_of_sample, slot_county):
    owners = lax.axis_size("samp")
    hour_count = lax.axis_size("hour")
    owner_index = lax.axis_index("samp")
    hour_index = lax.axis_index("hour")
    use_count, hour_dev, samp_dev = profiles.shape
    per_owner = load_gap.shape[0]
    row_width = use_count * hour_dev
    share_len = samp_dev // hour_count
    space_count = float(per_owner * owners * row_width * hour_count)
    sample_count = float(use_count * samp_dev * owners)
    my_counties = lax.dynamic_index_in_dim(slot_county, owner_index, 0, keepdims=False)
    slots = jnp.arange(slot_county.shape[1], dtype=jnp.int32)
    county = jnp.sum(
        jnp.where(slots[:, None] == slot_of_sample[None, :], my_counties[:, None], 0), axis=0
    )
    owner, row = county // per_owner, county % per_owner
    far = (owner // NY - owner_index // NY) % NZ
    beside = (owner % NY - owner_index % NY) % NY
    upper = (far * NY + beside) * HALF + row
    lower = ((NY + beside) * NZ + far) * HALF + row - HALF
    place = jnp.where(row < HALF, upper, lower)
    places = jnp.arange(owners * PAD, dtype=jnp.int32)
    onehot = (places[:, None] == place[None, :]).astype(jnp.bfloat16)
    wide = profiles.astype(jnp.float32)

    def padded(rows):
        return jnp.pad(rows, ((0, PAD - per_owner), (0, 0)))

    def backward(rows, number):
        everyone = everyone_of(padded(rows), number)
        square = jnp.sum(everyone * everyone)
        pieces = two_pieces(everyone, 1)
        spread = lax.dot_general(
            pieces, onehot, (((0,), (0,)), ((), ())), preferred_element_type=jnp.float32
        )
        spread = (spread[:row_width] + spread[row_width:]).reshape(use_count, hour_dev, samp_dev)
        partial = jnp.sum(wide * spread, axis=1)
        rest = jnp.full((8, 128), square)
        total = hour_total(jnp.concatenate([partial.reshape(-1, 128), rest], axis=0), number + 1)
        return total[:-8].reshape(use_count, samp_dev), total[-1, 0]

    def my_share(x):
        return lax.dynamic_slice_in_dim(x, hour_index * share_len, share_len, 1)

    gap_rows = load_gap.reshape(per_owner, row_width)
    plain, gap_total = backward(gap_rows, 1)
    beta_one = jnp.sqrt(gap_total / space_count + epsilon)
    image = plain / beta_one
    weighted = (wide * image[:, None, :]).reshape(row_width, samp_dev)
    sums = lax.dot_general(
        onehot, two_pieces(weighted, 0), (((1,), (1,)), ((), ())), preferred_element_type=jnp.float32
    )
    sums = (sums[:, :row_width] + sums[:, row_width:]).reshape(2 * owners, HALF, row_width)
    mine = jnp.sum(image * image)
    side = jnp.arange(2 * owners, dtype=jnp.int32)[:, None, None]
    line = jnp.arange(HALF, dtype=jnp.int32)[None, :, None]
    sums = jnp.where((side >= owners) & (line == per_owner - HALF), mine, sums)
    owned = owned_of(sums, 5)
    alpha_one = jnp.sqrt(owned[per_owner, 0] / sample_count + epsilon)
    mismatch = owned[:per_owner] / alpha_one - (alpha_one / beta_one) * gap_rows
    back, mismatch_total = backward(mismatch, 3)
    beta_two = jnp.sqrt(mismatch_total / space_count + epsilon)
    load_dir = mismatch / beta_two
    vector_one = image / alpha_one
    image_two = back / beta_two - beta_two * vector_one
    second_total = samp_total(jnp.full((8, 128), jnp.sum(image_two * image_two)), 6)[0, 0]
    alpha_two = jnp.sqrt(second_total / sample_count + epsilon)
    rho_value = jnp.sqrt(alpha_one * alpha_one + beta_two * beta_two)
    cosine = alpha_one / rho_value
    sine = beta_two / rho_value
    vector_share = my_share(vector_one)
    weight_step = cosine * beta_one / rho_value * vector_share
    search_dir = my_share(image_two) / alpha_two - sine * alpha_two / rho_value * vector_share
    return (weight_step, search_dir, load_dir.reshape(per_owner, use_count, hour_dev))


def solution(mesh):
    return jax.shard_map(
        local,
        mesh=mesh,
        in_specs=(P("samp", None, "hour"), P(None, "hour", "samp"), P("samp"), P()),
        out_specs=(P(None, ("samp", "hour")), P(None, ("samp", "hour")), P("samp", None, "hour")),
        check_vma=False,
    )
```

```python
import jax
import jax.numpy as jnp
from jax import lax
from jax.experimental import pallas as pl
from jax.experimental.pallas import tpu as pltpu
from jax.sharding import PartitionSpec as P

epsilon = 1e-06
PAD = 48
MESH = pl.DeviceIdType.MESH
NY = 4
NZ = 16
UP = NZ // 2
DOWN = NZ - 1 - UP


def remote(src, dst, send_sem, recv_sem, **device):
    return pltpu.make_async_remote_copy(
        src_ref=src, dst_ref=dst, send_sem=send_sem, recv_sem=recv_sem,
        device_id=device, device_id_type=MESH,
    )


def at_place(z, y):
    return lax.rem(z + NZ, NZ) * NY + lax.rem(y + NY, NY)


def greet(axis, peers):
    barrier = pltpu.get_barrier_semaphore()
    for peer in peers:
        pl.semaphore_signal(barrier, inc=1, device_id={axis: peer}, device_id_type=MESH)
    return len(peers)


def near_peers(z, y):
    return [at_place(z, y + d) for d in range(1, NY)] + [at_place(z + 1, y), at_place(z - 1, y)]


def gather_body(in_ref, out_ref, send_y, recv_y, send_z, recv_z):
    me = lax.axis_index("samp")
    z, y = me // NY, lax.rem(me, NY)

    def y_copy(d):
        return remote(in_ref, out_ref.at[me], send_y.at[d], recv_y.at[d], samp=at_place(z, y + d))

    def y_arrival(d):
        slot = out_ref.at[at_place(z, y - d)]
        return remote(slot, slot, send_y.at[d], recv_y.at[d], samp=at_place(z, y + d))

    def z_copy(way, k, j, own=False):
        step = 1 - 2 * way
        slot = out_ref.at[at_place(z - step * k, y - j)]
        return remote(
            in_ref if own else slot, slot, send_z.at[way, k, j], recv_z.at[way, k, j],
            samp=at_place(z + step, y),
        )

    def z_arrival(way, k, j):
        step = 1 - 2 * way
        slot = out_ref.at[at_place(z - step * (k + 1), y - j)]
        return remote(slot, slot, send_z.at[way, k, j], recv_z.at[way, k, j], samp=at_place(z + step, y))

    z_copy(0, 0, 0, True).start()
    z_copy(1, 0, 0, True).start()
    for d in (2, 1, 3):
        y_copy(d).start()
    out_ref[pl.ds(me, 1)] = in_ref[...][None]
    for j in (1, 3, 2):
        y_arrival(j).wait_recv()
        z_copy(0, 0, j).start()
        z_copy(1, 0, j).start()

    def hop(k, carry):
        for j in (0, 1, 3, 2):
            for way in (0, 1):
                z_arrival(way, k - 1, j).wait_recv()
                z_copy(way, k, j).start()
        return carry

    lax.fori_loop(1, DOWN, hop, 0)
    for j in (0, 1, 3, 2):
        z_arrival(0, UP - 2, j).wait_recv()
        z_copy(0, UP - 1, j).start()
        z_arrival(1, DOWN - 1, j).wait_recv()
    for d in (2, 1, 3):
        y_copy(d).wait_send()
    z_copy(0, 0, 0, True).wait_send()
    z_copy(1, 0, 0, True).wait_send()
    for j in (1, 3, 2):
        z_copy(0, 0, j).wait_send()
        z_copy(1, 0, j).wait_send()

    def drain(k, carry):
        for j in (0, 1, 3, 2):
            for way in (0, 1):
                z_copy(way, k, j).wait_send()
        return carry

    lax.fori_loop(1, DOWN, drain, 0)
    for j in (0, 1, 3, 2):
        z_copy(0, UP - 1, j).wait_send()
        z_arrival(0, UP - 1, j).wait_recv()


def gather_kernel(in_ref, out_ref, got, send_y, recv_y, send_z, recv_z):
    me = lax.axis_index("samp")
    z, y = me // NY, lax.rem(me, NY)
    pl.semaphore_wait(pltpu.get_barrier_semaphore(), greet("samp", near_peers(z, y)))
    gather_body(in_ref, got, send_y, recv_y, send_z, recv_z)
    out_ref[...] = got[...]


def vmem(count):
    return [pl.BlockSpec(memory_space=pltpu.VMEM)] * count


def everyone_of(rows, number):
    count = NY * NZ
    dma = pltpu.SemaphoreType.DMA
    return pl.pallas_call(
        gather_kernel,
        out_shape=jax.ShapeDtypeStruct((count, *rows.shape), jnp.float32),
        in_specs=vmem(1),
        out_specs=vmem(1)[0],
        scratch_shapes=[
            pltpu.VMEM((count, *rows.shape), jnp.float32),
            dma((NY,)), dma((NY,)), dma((2, UP, NY)), dma((2, UP, NY)),
        ],
        compiler_params=pltpu.CompilerParams(collective_id=number, has_side_effects=True),
    )(rows).reshape(count * rows.shape[0], rows.shape[1])


def scatter_body(in_ref, out_ref, held, total, arrived, send_y, recv_y, send_z, recv_z):
    me = lax.axis_index("samp")
    z, y = me // NY, lax.rem(me, NY)
    order = (2, 1, 3, 0)

    def z_copy(way, k, j, own=False):
        step = 1 - 2 * way
        far = (UP, DOWN)[way] - k
        src = in_ref.at[at_place(z + step * far, y + j)] if own else held.at[way, k - 1, j]
        return remote(
            src, held.at[way, k, j], send_z.at[way, k, j], recv_z.at[way, k, j],
            samp=at_place(z + step, y),
        )

    def z_arrival(way, k, j):
        step = 1 - 2 * way
        slot = held.at[way, k, j]
        return remote(slot, slot, send_z.at[way, k, j], recv_z.at[way, k, j], samp=at_place(z + step, y))

    def add_own(way, k, j):
        step = 1 - 2 * way
        far = (UP, DOWN)[way] - k
        z_arrival(way, k - 1, j).wait_recv()
        held[way, k - 1, j] = held[way, k - 1, j] + in_ref[at_place(z + step * far, y + j)]
        z_copy(way, k, j).start()

    def y_copy(d):
        return remote(total.at[d], arrived.at[d], send_y.at[d], recv_y.at[d], samp=at_place(z, y + d))

    for j in order:
        for way in (0, 1):
            z_copy(way, 0, j, True).start()

    def hop(k, carry):
        for j in order:
            for way in (0, 1):
                add_own(way, k, j)
        return carry

    lax.fori_loop(1, DOWN, hop, 0)
    for j in order:
        add_own(0, UP - 1, j)
    for j in order:
        z_arrival(1, DOWN - 1, j).wait_recv()
        z_arrival(0, UP - 1, j).wait_recv()
        total[j] = held[0, UP - 1, j] + held[1, DOWN - 1, j] + in_ref[at_place(z, y + j)]
        if j:
            y_copy(j).start()

    def drain(k, carry):
        for j in order:
            for way in (0, 1):
                z_copy(way, k, j).wait_send()
        return carry

    for j in order:
        for way in (0, 1):
            z_copy(way, 0, j, True).wait_send()
    lax.fori_loop(1, DOWN, drain, 0)
    for j in order:
        z_copy(0, UP - 1, j).wait_send()
    for d in (1, 3, 2):
        y_copy(d).wait()
    out_ref[...] = total[0] + arrived[1] + arrived[2] + arrived[3]


def middle_kernel(sample_count, real, in_ref, gap_ref, beta_ref, all_ref, mine_ref, owned, fresh, got, *rest):
    me = lax.axis_index("samp")
    z, y = me // NY, lax.rem(me, NY)
    pl.semaphore_wait(pltpu.get_barrier_semaphore(), greet("samp", near_peers(z, y)))
    scatter_body(in_ref, owned, *rest[:7])
    alpha_one = jnp.sqrt(owned[pl.ds(real, 1)] / sample_count + epsilon)
    beta_one = beta_ref[pl.ds(0, 1)]
    mismatch = owned[...] / alpha_one - (alpha_one / beta_one) * gap_ref[...]
    row = lax.broadcasted_iota(jnp.int32, mismatch.shape, 0)
    mismatch = jnp.where(row < real, mismatch, 0.0)
    fresh[...] = mismatch
    mine_ref[pl.ds(0, PAD)] = mismatch
    mine_ref[pl.ds(PAD, 8)] = jnp.broadcast_to(alpha_one, (8, 128))
    gather_body(fresh, got, *rest[7:])
    all_ref[...] = got[...]


def middle(sums, gap, beta, sample_count, real, number):
    block = sums.shape[1:]
    dma = pltpu.SemaphoreType.DMA
    sems = [dma((NY,)), dma((NY,)), dma((2, UP, NY)), dma((2, UP, NY))]
    return pl.pallas_call(
        lambda *refs: middle_kernel(sample_count, real, *refs),
        out_shape=[
            jax.ShapeDtypeStruct(sums.shape, jnp.float32),
            jax.ShapeDtypeStruct((PAD + 8, block[1]), jnp.float32),
        ],
        in_specs=vmem(3),
        out_specs=vmem(2),
        scratch_shapes=[
            pltpu.VMEM(block, jnp.float32),
            pltpu.VMEM(block, jnp.float32),
            pltpu.VMEM(sums.shape, jnp.float32),
            pltpu.VMEM((2, UP, NY, *block), jnp.float32),
            pltpu.VMEM((NY, *block), jnp.float32),
            pltpu.VMEM((NY, *block), jnp.float32),
            *sems, *sems,
        ],
        compiler_params=pltpu.CompilerParams(collective_id=number, has_side_effects=True),
    )(sums, gap, beta)


def hour_kernel(n, in_ref, out_ref, arrived, send_sem, recv_sem):
    me = lax.axis_index("hour")
    order = [n // 2] + [d for d in range(1, n) if d != n // 2]

    def copy(d):
        return remote(in_ref, arrived.at[d], send_sem.at[d], recv_sem.at[d], hour=lax.rem(me + d, n))

    peers = [lax.rem(me + d, n) for d in order]
    pl.semaphore_wait(pltpu.get_barrier_semaphore(), greet("hour", peers))
    for d in order:
        copy(d).start()
    arrived[0] = in_ref[...]
    for d in order:
        copy(d).wait()
    out_ref[...] = jnp.sum(arrived[...], axis=0)


def hour_total(x, number):
    n = lax.axis_size("hour")
    dma = pltpu.SemaphoreType.DMA
    return pl.pallas_call(
        lambda *refs: hour_kernel(n, *refs),
        out_shape=jax.ShapeDtypeStruct(x.shape, jnp.float32),
        in_specs=vmem(1),
        out_specs=vmem(1)[0],
        scratch_shapes=[pltpu.VMEM((n, *x.shape), jnp.float32), dma((n,)), dma((n,))],
        compiler_params=pltpu.CompilerParams(collective_id=number, has_side_effects=True),
    )(x)


def last_kernel(
    n, space_count, in_ref, vector_ref, out_ref, arrived, first, middle, second, start,
    send_h, recv_h, send_y, recv_y, send_z, recv_z,
):
    me, hour = lax.axis_index("samp"), lax.axis_index("hour")
    z, y = me // NY, lax.rem(me, NY)
    order = [n // 2] + [d for d in range(1, n) if d != n // 2]
    far_first = sorted(range(1, NZ), key=lambda d: -min(d, NZ - d))
    rows = vector_ref.shape[0]

    def h_copy(d):
        return remote(in_ref, arrived.at[d], send_h.at[d], recv_h.at[d], hour=lax.rem(hour + d, n))

    def y_copy(d):
        return remote(start, first.at[d], send_y.at[d], recv_y.at[d], samp=at_place(z, y + d))

    def z_copy(d):
        return remote(middle, second.at[d], send_z.at[d], recv_z.at[d], samp=at_place(z + d, y))

    peers = [at_place(z + d, y) for d in far_first] + [at_place(z, y + d) for d in (2, 1, 3)]
    count = greet("samp", peers) + greet("hour", [lax.rem(hour + d, n) for d in order])
    pl.semaphore_wait(pltpu.get_barrier_semaphore(), count)
    for d in order:
        h_copy(d).start()
    arrived[0] = in_ref[...]
    for d in order:
        h_copy(d).wait()
    total = jnp.sum(arrived[...], axis=0)
    square = total[rows:]
    beta_two = jnp.sqrt(square[:1] / space_count + epsilon)
    image_two = total[:rows] / beta_two - beta_two * vector_ref[...]
    out_ref[pl.ds(0, rows)] = image_two
    out_ref[pl.ds(rows, 8)] = square
    start[...] = jnp.full(start.shape, jnp.sum(image_two * image_two))
    for d in (2, 1, 3):
        y_copy(d).start()
    first[0] = start[...]
    for d in (1, 3, 2):
        y_copy(d).wait()
    middle[...] = jnp.sum(first[...], axis=0)
    for d in far_first:
        z_copy(d).start()
    second[0] = middle[...]
    for d in far_first[::-1]:
        z_copy(d).wait()
    out_ref[pl.ds(rows + 8, 8)] = jnp.sum(second[...], axis=0)


def last_sums(x, vector, space_count, number):
    n = lax.axis_size("hour")
    dma = pltpu.SemaphoreType.DMA
    small = (8, 128)
    return pl.pallas_call(
        lambda *refs: last_kernel(n, space_count, *refs),
        out_shape=jax.ShapeDtypeStruct((x.shape[0] + 8, 128), jnp.float32),
        in_specs=vmem(2),
        out_specs=vmem(1)[0],
        scratch_shapes=[
            pltpu.VMEM((n, *x.shape), jnp.float32),
            pltpu.VMEM((NY, *small), jnp.float32),
            pltpu.VMEM(small, jnp.float32),
            pltpu.VMEM((NZ, *small), jnp.float32),
            pltpu.VMEM(small, jnp.float32),
            dma((n,)), dma((n,)), dma((NY,)), dma((NY,)), dma((NZ,)), dma((NZ,)),
        ],
        compiler_params=pltpu.CompilerParams(collective_id=number, has_side_effects=True),
    )(x, vector)


def two_pieces(x, axis):
    high = lax.reduce_precision(x, 8, 7)
    return jnp.concatenate([high, x - high], axis=axis).astype(jnp.bfloat16)


def local(load_gap, profiles, slot_of_sample, slot_county):
    owners = lax.axis_size("samp")
    hour_count = lax.axis_size("hour")
    owner_index = lax.axis_index("samp")
    hour_index = lax.axis_index("hour")
    use_count, hour_dev, samp_dev = profiles.shape
    per_owner = load_gap.shape[0]
    row_width = use_count * hour_dev
    share_len = samp_dev // hour_count
    space_count = float(per_owner * owners * row_width * hour_count)
    sample_count = float(use_count * samp_dev * owners)
    my_counties = lax.dynamic_index_in_dim(slot_county, owner_index, 0, keepdims=False)
    slots = jnp.arange(slot_county.shape[1], dtype=jnp.int32)
    county = jnp.sum(
        jnp.where(slots[:, None] == slot_of_sample[None, :], my_counties[:, None], 0), axis=0
    )
    place = county // per_owner * PAD + county % per_owner
    places = jnp.arange(owners * PAD, dtype=jnp.int32)
    onehot = (places[:, None] == place[None, :]).astype(jnp.bfloat16)
    wide = profiles.astype(jnp.float32)

    def padded(rows):
        return jnp.pad(rows, ((0, PAD - per_owner), (0, 0)))

    def backward(everyone):
        everyone = everyone.reshape(-1, row_width)
        square = jnp.sum(everyone * everyone)
        pieces = two_pieces(everyone, 1)
        spread = lax.dot_general(
            pieces, onehot, (((0,), (0,)), ((), ())), preferred_element_type=jnp.float32
        )
        spread = (spread[:row_width] + spread[row_width:]).reshape(use_count, hour_dev, samp_dev)
        partial = jnp.sum(wide * spread, axis=1)
        return jnp.concatenate([partial.reshape(-1, 128), jnp.full((8, 128), square)], axis=0)

    def my_share(x):
        return lax.dynamic_slice_in_dim(x, hour_index * share_len, share_len, 1)

    gap_rows = load_gap.reshape(per_owner, row_width)
    total = hour_total(backward(everyone_of(padded(gap_rows), 1)), 2)
    plain, gap_total = total[:-8].reshape(use_count, samp_dev), total[-1, 0]
    beta_one = jnp.sqrt(gap_total / space_count + epsilon)
    image = plain / beta_one
    weighted = (wide * image[:, None, :]).reshape(row_width, samp_dev)
    sums = lax.dot_general(
        onehot, two_pieces(weighted, 0), (((1,), (1,)), ((), ())), preferred_element_type=jnp.float32
    )
    sums = (sums[:, :row_width] + sums[:, row_width:]).reshape(owners, PAD, row_width)
    mine = jnp.sum(image * image)
    row = jnp.arange(PAD, dtype=jnp.int32)[None, :, None]
    sums = jnp.where(row == per_owner, mine, sums)
    everyone, owned = middle(
        sums, padded(gap_rows), jnp.full((8, 128), beta_one), sample_count, per_owner, 3
    )
    mismatch, alpha_one = owned[:per_owner], owned[PAD, 0]
    vector_one = image / alpha_one
    last = last_sums(backward(everyone), vector_one.reshape(-1, 128), space_count, 4)
    beta_two = jnp.sqrt(last[-16, 0] / space_count + epsilon)
    alpha_two = jnp.sqrt(last[-1, 0] / sample_count + epsilon)
    image_two = last[:-16].reshape(use_count, samp_dev)
    load_dir = mismatch / beta_two
    rho_value = jnp.sqrt(alpha_one * alpha_one + beta_two * beta_two)
    cosine = alpha_one / rho_value
    sine = beta_two / rho_value
    vector_share = my_share(vector_one)
    weight_step = cosine * beta_one / rho_value * vector_share
    search_dir = my_share(image_two) / alpha_two - sine * alpha_two / rho_value * vector_share
    return (weight_step, search_dir, load_dir.reshape(per_owner, use_count, hour_dev))


def solution(mesh):
    return jax.shard_map(
        local,
        mesh=mesh,
        in_specs=(P("samp", None, "hour"), P(None, "hour", "samp"), P("samp"), P()),
        out_specs=(P(None, ("samp", "hour")), P(None, ("samp", "hour")), P("samp", None, "hour")),
        check_vma=False,
    )
```

```python
import jax
import jax.numpy as jnp
from jax import lax
from jax.experimental import pallas as pl
from jax.experimental.pallas import tpu as pltpu
from jax.sharding import PartitionSpec as P

epsilon = 1e-06
PAD = 48
MESH = pl.DeviceIdType.MESH
NY = 4
NZ = 16
UP = NZ // 2
DOWN = NZ - 1 - UP


def remote(src, dst, send_sem, recv_sem, **device):
    return pltpu.make_async_remote_copy(
        src_ref=src, dst_ref=dst, send_sem=send_sem, recv_sem=recv_sem,
        device_id=device, device_id_type=MESH,
    )


def at_place(z, y):
    return lax.rem(z + NZ, NZ) * NY + lax.rem(y + NY, NY)


def greet(axis, peers):
    barrier = pltpu.get_barrier_semaphore()
    for peer in peers:
        pl.semaphore_signal(barrier, inc=1, device_id={axis: peer}, device_id_type=MESH)
    return len(peers)


def near_peers(z, y):
    return [at_place(z, y + d) for d in range(1, NY)] + [at_place(z + 1, y), at_place(z - 1, y)]


def gather_body(use, in_ref, out_ref, send_y, recv_y, send_z, recv_z):
    me = lax.axis_index("samp")
    z, y = me // NY, lax.rem(me, NY)

    def y_copy(d):
        return remote(in_ref, out_ref.at[me], send_y.at[d], recv_y.at[d], samp=at_place(z, y + d))

    def y_arrival(d):
        slot = out_ref.at[at_place(z, y - d)]
        return remote(slot, slot, send_y.at[d], recv_y.at[d], samp=at_place(z, y + d))

    def z_copy(way, k, j, own=False):
        step = 1 - 2 * way
        slot = out_ref.at[at_place(z - step * k, y - j)]
        return remote(
            in_ref if own else slot, slot, send_z.at[way, k, j], recv_z.at[way, k, j],
            samp=at_place(z + step, y),
        )

    def z_arrival(way, k, j):
        step = 1 - 2 * way
        slot = out_ref.at[at_place(z - step * (k + 1), y - j)]
        return remote(slot, slot, send_z.at[way, k, j], recv_z.at[way, k, j], samp=at_place(z + step, y))

    z_copy(0, 0, 0, True).start()
    z_copy(1, 0, 0, True).start()
    for d in (2, 1, 3):
        y_copy(d).start()
    out_ref[pl.ds(me, 1)] = in_ref[...][None]
    for j in (1, 3, 2):
        y_arrival(j).wait_recv()
        z_copy(0, 0, j).start()
        z_copy(1, 0, j).start()
    use(z)

    def hop(k, carry):
        for j in (0, 1, 3, 2):
            for way in (0, 1):
                z_arrival(way, k - 1, j).wait_recv()
                z_copy(way, k, j).start()
        use(lax.rem(z + NZ - k, NZ))
        use(lax.rem(z + k, NZ))
        return carry

    lax.fori_loop(1, DOWN, hop, 0)
    for j in (0, 1, 3, 2):
        z_arrival(0, UP - 2, j).wait_recv()
        z_copy(0, UP - 1, j).start()
        z_arrival(1, DOWN - 1, j).wait_recv()
    use(lax.rem(z + NZ - DOWN, NZ))
    use(lax.rem(z + DOWN, NZ))
    for d in (2, 1, 3):
        y_copy(d).wait_send()
    z_copy(0, 0, 0, True).wait_send()
    z_copy(1, 0, 0, True).wait_send()
    for j in (1, 3, 2):
        z_copy(0, 0, j).wait_send()
        z_copy(1, 0, j).wait_send()

    def drain(k, carry):
        for j in (0, 1, 3, 2):
            for way in (0, 1):
                z_copy(way, k, j).wait_send()
        return carry

    lax.fori_loop(1, DOWN, drain, 0)
    for j in (0, 1, 3, 2):
        z_copy(0, UP - 1, j).wait_send()
        z_arrival(0, UP - 1, j).wait_recv()
    use(lax.rem(z + NZ - UP, NZ))


def spread_into(acc, square, got, place_ref):
    bundle = NY * PAD
    acc[...] = jnp.zeros_like(acc)
    square[...] = jnp.zeros_like(square)

    def use(z):
        block = got[pl.ds(z * NY, NY)].reshape(bundle, 128)
        high = block.astype(jnp.bfloat16)
        low = (block - high.astype(jnp.float32)).astype(jnp.bfloat16)
        both = jnp.concatenate([high, low], axis=1)
        places = lax.broadcasted_iota(jnp.int32, (bundle, place_ref.shape[1]), 0) + z * bundle
        hit = jnp.where(places == place_ref[...], 1.0, 0.0).astype(jnp.bfloat16)
        acc[...] += lax.dot_general(
            both, hit, (((0,), (0,)), ((), ())), preferred_element_type=jnp.float32
        )
        square[...] += jnp.sum((block * block).reshape(bundle // 8, 8, 128), axis=0)

    return use


def fold(acc, square, prof_ref, part):
    uses, hours, width = prof_ref.shape
    for e in range(uses):
        here = acc[pl.ds(e * hours, hours)] + acc[pl.ds((uses + e) * hours, hours)]
        line = jnp.sum(here * prof_ref[e].astype(jnp.float32), axis=0, keepdims=True)
        for c in range(width // 128):
            part[pl.ds(e * (width // 128) + c, 1)] = line[:, c * 128:(c + 1) * 128]
    part[pl.ds(uses * width // 128, 8)] = jnp.full((8, 128), jnp.sum(square[...]))


def hour_peers(n):
    return [n // 2] + [d for d in range(1, n) if d != n // 2]


def hour_body(n, part, arrived, send_h, recv_h):
    me = lax.axis_index("hour")

    def copy(d):
        return remote(part, arrived.at[d], send_h.at[d], recv_h.at[d], hour=lax.rem(me + d, n))

    for d in hour_peers(n):
        copy(d).start()
    arrived[0] = part[...]
    for d in hour_peers(n):
        copy(d).wait()
    return jnp.sum(arrived[...], axis=0)


def greet_hours(n):
    hour = lax.axis_index("hour")
    return greet("hour", [lax.rem(hour + d, n) for d in hour_peers(n)])


def first_kernel(n, in_ref, place_ref, prof_ref, out_ref, got, acc, square, part, arrived, *sems):
    me = lax.axis_index("samp")
    z, y = me // NY, lax.rem(me, NY)
    count = greet("samp", near_peers(z, y)) + greet_hours(n)
    pl.semaphore_wait(pltpu.get_barrier_semaphore(), count)
    gather_body(spread_into(acc, square, got, place_ref), in_ref, got, *sems[:4])
    fold(acc, square, prof_ref, part)
    out_ref[...] = hour_body(n, part, arrived, *sems[4:])


def vmem(count):
    return [pl.BlockSpec(memory_space=pltpu.VMEM)] * count


def gather_sems():
    dma = pltpu.SemaphoreType.DMA
    return [dma((NY,)), dma((NY,)), dma((2, UP, NY)), dma((2, UP, NY))]


def spread_scratch(n, width, uses):
    part = (uses * width // 128 + 8, 128)
    return [
        pltpu.VMEM((NY * NZ, PAD, 128), jnp.float32),
        pltpu.VMEM((256, width), jnp.float32),
        pltpu.VMEM((8, 128), jnp.float32),
        pltpu.VMEM(part, jnp.float32),
        pltpu.VMEM((n, *part), jnp.float32),
    ]


def first_total(rows, place, profiles, number):
    n = lax.axis_size("hour")
    uses, _, width = profiles.shape
    dma = pltpu.SemaphoreType.DMA
    return pl.pallas_call(
        lambda *refs: first_kernel(n, *refs),
        out_shape=jax.ShapeDtypeStruct((uses * width // 128 + 8, 128), jnp.float32),
        in_specs=vmem(3),
        out_specs=vmem(1)[0],
        scratch_shapes=[*spread_scratch(n, width, uses), *gather_sems(), dma((n,)), dma((n,))],
        compiler_params=pltpu.CompilerParams(collective_id=number, has_side_effects=True),
    )(rows, place, profiles)


def scatter_body(in_ref, out_ref, held, total, arrived, send_y, recv_y, send_z, recv_z):
    me = lax.axis_index("samp")
    z, y = me // NY, lax.rem(me, NY)
    order = (2, 1, 3, 0)

    def z_copy(way, k, j, own=False):
        step = 1 - 2 * way
        far = (UP, DOWN)[way] - k
        src = in_ref.at[at_place(z + step * far, y + j)] if own else held.at[way, k - 1, j]
        return remote(
            src, held.at[way, k, j], send_z.at[way, k, j], recv_z.at[way, k, j],
            samp=at_place(z + step, y),
        )

    def z_arrival(way, k, j):
        step = 1 - 2 * way
        slot = held.at[way, k, j]
        return remote(slot, slot, send_z.at[way, k, j], recv_z.at[way, k, j], samp=at_place(z + step, y))

    def add_own(way, k, j):
        step = 1 - 2 * way
        far = (UP, DOWN)[way] - k
        z_arrival(way, k - 1, j).wait_recv()
        held[way, k - 1, j] = held[way, k - 1, j] + in_ref[at_place(z + step * far, y + j)]
        z_copy(way, k, j).start()

    def y_copy(d):
        return remote(total.at[d], arrived.at[d], send_y.at[d], recv_y.at[d], samp=at_place(z, y + d))

    for j in order:
        for way in (0, 1):
            z_copy(way, 0, j, True).start()

    def hop(k, carry):
        for j in order:
            for way in (0, 1):
                add_own(way, k, j)
        return carry

    lax.fori_loop(1, DOWN, hop, 0)
    for j in order:
        add_own(0, UP - 1, j)
    for j in order:
        z_arrival(1, DOWN - 1, j).wait_recv()
        z_arrival(0, UP - 1, j).wait_recv()
        total[j] = held[0, UP - 1, j] + held[1, DOWN - 1, j] + in_ref[at_place(z, y + j)]
        if j:
            y_copy(j).start()

    def drain(k, carry):
        for j in order:
            for way in (0, 1):
                z_copy(way, k, j).wait_send()
        return carry

    for j in order:
        for way in (0, 1):
            z_copy(way, 0, j, True).wait_send()
    lax.fori_loop(1, DOWN, drain, 0)
    for j in order:
        z_copy(0, UP - 1, j).wait_send()
    for d in (1, 3, 2):
        y_copy(d).wait()
    out_ref[...] = total[0] + arrived[1] + arrived[2] + arrived[3]


def second_kernel(
    n, sample_count, space_count, real,
    in_ref, gap_ref, beta_ref, image_ref, place_ref, prof_ref, mine_ref, out_ref,
    got, acc, square, part, arrived, owned, fresh, held, total, landed, first, middle, second, start,
    *sems,
):
    me = lax.axis_index("samp")
    z, y = me // NY, lax.rem(me, NY)
    far_first = sorted(range(1, NZ), key=lambda d: -min(d, NZ - d))
    rows = image_ref.shape[0]
    send_y, recv_y, send_z, recv_z = sems[10:]

    def y_copy(d):
        return remote(start, first.at[d], send_y.at[d], recv_y.at[d], samp=at_place(z, y + d))

    def z_copy(d):
        return remote(middle, second.at[d], send_z.at[d], recv_z.at[d], samp=at_place(z + d, y))

    peers = [at_place(z + d, y) for d in far_first] + [at_place(z, y + d) for d in (2, 1, 3)]
    count = greet("samp", peers) + greet_hours(n)
    pl.semaphore_wait(pltpu.get_barrier_semaphore(), count)
    scatter_body(in_ref, owned, held, total, landed, *sems[:4])
    alpha_one = jnp.sqrt(owned[pl.ds(real, 1)] / sample_count + epsilon)
    beta_one = beta_ref[pl.ds(0, 1)]
    mismatch = owned[...] / alpha_one - (alpha_one / beta_one) * gap_ref[...]
    row = lax.broadcasted_iota(jnp.int32, mismatch.shape, 0)
    mismatch = jnp.where(row < real, mismatch, 0.0)
    fresh[...] = mismatch
    mine_ref[pl.ds(0, PAD)] = mismatch
    mine_ref[pl.ds(PAD, 8)] = jnp.broadcast_to(alpha_one, (8, 128))
    gather_body(spread_into(acc, square, got, place_ref), fresh, got, *sems[4:8])
    fold(acc, square, prof_ref, part)
    whole = hour_body(n, part, arrived, *sems[8:10])
    beta_two = jnp.sqrt(whole[rows:rows + 1] / space_count + epsilon)
    image_two = whole[:rows] / beta_two - beta_two * (image_ref[...] / alpha_one)
    out_ref[pl.ds(0, rows)] = image_two
    out_ref[pl.ds(rows, 8)] = whole[rows:]
    start[...] = jnp.full(start.shape, jnp.sum(image_two * image_two))
    for d in (2, 1, 3):
        y_copy(d).start()
    first[0] = start[...]
    for d in (1, 3, 2):
        y_copy(d).wait()
    middle[...] = jnp.sum(first[...], axis=0)
    for d in far_first:
        z_copy(d).start()
    second[0] = middle[...]
    for d in far_first[::-1]:
        z_copy(d).wait()
    out_ref[pl.ds(rows + 8, 8)] = jnp.sum(second[...], axis=0)


def second_totals(sums, gap, beta, image, place, profiles, sample_count, space_count, real, number):
    n = lax.axis_size("hour")
    uses, _, width = profiles.shape
    block, small = sums.shape[1:], (8, 128)
    dma = pltpu.SemaphoreType.DMA
    return pl.pallas_call(
        lambda *refs: second_kernel(n, sample_count, space_count, real, *refs),
        out_shape=[
            jax.ShapeDtypeStruct((PAD + 8, block[1]), jnp.float32),
            jax.ShapeDtypeStruct((image.shape[0] + 16, 128), jnp.float32),
        ],
        in_specs=vmem(6),
        out_specs=vmem(2),
        scratch_shapes=[
            *spread_scratch(n, width, uses),
            pltpu.VMEM(block, jnp.float32),
            pltpu.VMEM(block, jnp.float32),
            pltpu.VMEM((2, UP, NY, *block), jnp.float32),
            pltpu.VMEM((NY, *block), jnp.float32),
            pltpu.VMEM((NY, *block), jnp.float32),
            pltpu.VMEM((NY, *small), jnp.float32),
            pltpu.VMEM(small, jnp.float32),
            pltpu.VMEM((NZ, *small), jnp.float32),
            pltpu.VMEM(small, jnp.float32),
            *gather_sems(), *gather_sems(), dma((n,)), dma((n,)),
            dma((NY,)), dma((NY,)), dma((NZ,)), dma((NZ,)),
        ],
        compiler_params=pltpu.CompilerParams(collective_id=number, has_side_effects=True),
    )(sums, gap, beta, image, place, profiles)


def two_pieces(x, axis):
    high = lax.reduce_precision(x, 8, 7)
    return jnp.concatenate([high, x - high], axis=axis).astype(jnp.bfloat16)


def local(load_gap, profiles, slot_of_sample, slot_county):
    owners = lax.axis_size("samp")
    hour_count = lax.axis_size("hour")
    owner_index = lax.axis_index("samp")
    hour_index = lax.axis_index("hour")
    use_count, hour_dev, samp_dev = profiles.shape
    per_owner = load_gap.shape[0]
    row_width = use_count * hour_dev
    share_len = samp_dev // hour_count
    space_count = float(per_owner * owners * row_width * hour_count)
    sample_count = float(use_count * samp_dev * owners)
    my_counties = lax.dynamic_index_in_dim(slot_county, owner_index, 0, keepdims=False)
    slots = jnp.arange(slot_county.shape[1], dtype=jnp.int32)
    county = jnp.sum(
        jnp.where(slots[:, None] == slot_of_sample[None, :], my_counties[:, None], 0), axis=0
    )
    place = county // per_owner * PAD + county % per_owner
    places = jnp.arange(owners * PAD, dtype=jnp.int32)
    onehot = (places[:, None] == place[None, :]).astype(jnp.bfloat16)
    wide = profiles.astype(jnp.float32)

    def padded(rows):
        return jnp.pad(rows, ((0, PAD - per_owner), (0, 0)))

    def my_share(x):
        return lax.dynamic_slice_in_dim(x, hour_index * share_len, share_len, 1)

    gap_rows = load_gap.reshape(per_owner, row_width)
    total = first_total(padded(gap_rows), place[None], profiles, 1)
    plain, gap_total = total[:-8].reshape(use_count, samp_dev), total[-1, 0]
    beta_one = jnp.sqrt(gap_total / space_count + epsilon)
    image = plain / beta_one
    weighted = (wide * image[:, None, :]).reshape(row_width, samp_dev)
    sums = lax.dot_general(
        onehot, two_pieces(weighted, 0), (((1,), (1,)), ((), ())), preferred_element_type=jnp.float32
    )
    sums = (sums[:, :row_width] + sums[:, row_width:]).reshape(owners, PAD, row_width)
    mine = jnp.sum(image * image)
    row = jnp.arange(PAD, dtype=jnp.int32)[None, :, None]
    sums = jnp.where(row == per_owner, mine, sums)
    owned, last = second_totals(
        sums, padded(gap_rows), jnp.full((8, 128), beta_one), total[:-8] / beta_one, place[None],
        profiles, sample_count, space_count, per_owner, 2,
    )
    mismatch, alpha_one = owned[:per_owner], owned[PAD, 0]
    vector_one = image / alpha_one
    beta_two = jnp.sqrt(last[-16, 0] / space_count + epsilon)
    alpha_two = jnp.sqrt(last[-1, 0] / sample_count + epsilon)
    image_two = last[:-16].reshape(use_count, samp_dev)
    load_dir = mismatch / beta_two
    rho_value = jnp.sqrt(alpha_one * alpha_one + beta_two * beta_two)
    cosine = alpha_one / rho_value
    sine = beta_two / rho_value
    vector_share = my_share(vector_one)
    weight_step = cosine * beta_one / rho_value * vector_share
    search_dir = my_share(image_two) / alpha_two - sine * alpha_two / rho_value * vector_share
    return (weight_step, search_dir, load_dir.reshape(per_owner, use_count, hour_dev))


def solution(mesh):
    return jax.shard_map(
        local,
        mesh=mesh,
        in_specs=(P("samp", None, "hour"), P(None, "hour", "samp"), P("samp"), P()),
        out_specs=(P(None, ("samp", "hour")), P(None, ("samp", "hour")), P("samp", None, "hour")),
        check_vma=False,
    )
```

```python
import jax
import jax.numpy as jnp
from jax import lax
from jax.experimental import pallas as pl
from jax.experimental.pallas import tpu as pltpu
from jax.sharding import PartitionSpec as P

epsilon = 1e-06
PAD = 48
MESH = pl.DeviceIdType.MESH
NY = 4
NZ = 16
UP = NZ // 2
DOWN = NZ - 1 - UP


def remote(src, dst, send_sem, recv_sem, **device):
    return pltpu.make_async_remote_copy(
        src_ref=src, dst_ref=dst, send_sem=send_sem, recv_sem=recv_sem,
        device_id=device, device_id_type=MESH,
    )


def at_place(z, y):
    return lax.rem(z + NZ, NZ) * NY + lax.rem(y + NY, NY)


def greet(axis, peers):
    barrier = pltpu.get_barrier_semaphore()
    for peer in peers:
        pl.semaphore_signal(barrier, inc=1, device_id={axis: peer}, device_id_type=MESH)
    return len(peers)


def near_peers(z, y):
    return [at_place(z, y + d) for d in range(1, NY)] + [at_place(z + 1, y), at_place(z - 1, y)]


def gather_body(use, in_ref, out_ref, send_y, recv_y, send_z, recv_z):
    me = lax.axis_index("samp")
    z, y = me // NY, lax.rem(me, NY)

    def y_copy(d):
        return remote(in_ref, out_ref.at[me], send_y.at[d], recv_y.at[d], samp=at_place(z, y + d))

    def y_arrival(d):
        slot = out_ref.at[at_place(z, y - d)]
        return remote(slot, slot, send_y.at[d], recv_y.at[d], samp=at_place(z, y + d))

    def z_copy(way, k, j, own=False):
        step = 1 - 2 * way
        slot = out_ref.at[at_place(z - step * k, y - j)]
        return remote(
            in_ref if own else slot, slot, send_z.at[way, k, j], recv_z.at[way, k, j],
            samp=at_place(z + step, y),
        )

    def z_arrival(way, k, j):
        step = 1 - 2 * way
        slot = out_ref.at[at_place(z - step * (k + 1), y - j)]
        return remote(slot, slot, send_z.at[way, k, j], recv_z.at[way, k, j], samp=at_place(z + step, y))

    z_copy(0, 0, 0, True).start()
    z_copy(1, 0, 0, True).start()
    for d in (2, 1, 3):
        y_copy(d).start()
    out_ref[pl.ds(me, 1)] = in_ref[...][None]
    for j in (1, 3, 2):
        y_arrival(j).wait_recv()
        z_copy(0, 0, j).start()
        z_copy(1, 0, j).start()
    use(z)

    def hop(k, carry):
        for j in (0, 1, 3, 2):
            for way in (0, 1):
                z_arrival(way, k - 1, j).wait_recv()
                z_copy(way, k, j).start()
        use(lax.rem(z + NZ - k, NZ))
        use(lax.rem(z + k, NZ))
        return carry

    lax.fori_loop(1, DOWN, hop, 0)
    for j in (0, 1, 3, 2):
        z_arrival(0, UP - 2, j).wait_recv()
        z_copy(0, UP - 1, j).start()
        z_arrival(1, DOWN - 1, j).wait_recv()
    use(lax.rem(z + NZ - DOWN, NZ))
    use(lax.rem(z + DOWN, NZ))
    for d in (2, 1, 3):
        y_copy(d).wait_send()
    z_copy(0, 0, 0, True).wait_send()
    z_copy(1, 0, 0, True).wait_send()
    for j in (1, 3, 2):
        z_copy(0, 0, j).wait_send()
        z_copy(1, 0, j).wait_send()

    def drain(k, carry):
        for j in (0, 1, 3, 2):
            for way in (0, 1):
                z_copy(way, k, j).wait_send()
        return carry

    lax.fori_loop(1, DOWN, drain, 0)
    for j in (0, 1, 3, 2):
        z_copy(0, UP - 1, j).wait_send()
        z_arrival(0, UP - 1, j).wait_recv()
    use(lax.rem(z + NZ - UP, NZ))


def spread_into(acc, square, got, place_ref):
    bundle = NY * PAD
    acc[...] = jnp.zeros_like(acc)
    square[...] = jnp.zeros_like(square)

    def use(z):
        block = got[pl.ds(z * NY, NY)].reshape(bundle, 128)
        high = block.astype(jnp.bfloat16)
        low = (block - high.astype(jnp.float32)).astype(jnp.bfloat16)
        both = jnp.concatenate([high, low], axis=1)
        places = lax.broadcasted_iota(jnp.int32, (bundle, place_ref.shape[1]), 0) + z * bundle
        hit = jnp.where(places == place_ref[...], 1.0, 0.0).astype(jnp.bfloat16)
        acc[...] += lax.dot_general(
            both, hit, (((0,), (0,)), ((), ())), preferred_element_type=jnp.float32
        )
        square[...] += jnp.sum((block * block).reshape(bundle // 8, 8, 128), axis=0)

    return use


def fold(acc, square, prof_ref, part):
    uses, hours, width = prof_ref.shape
    for e in range(uses):
        here = acc[pl.ds(e * hours, hours)] + acc[pl.ds((uses + e) * hours, hours)]
        line = jnp.sum(here * prof_ref[e].astype(jnp.float32), axis=0, keepdims=True)
        for c in range(width // 128):
            part[pl.ds(e * (width // 128) + c, 1)] = line[:, c * 128:(c + 1) * 128]
    part[pl.ds(uses * width // 128, 8)] = jnp.full((8, 128), jnp.sum(square[...]))


def hour_peers(n):
    return [n // 2] + [d for d in range(1, n) if d != n // 2]


def hour_body(n, part, arrived, send_h, recv_h):
    me = lax.axis_index("hour")

    def copy(d):
        return remote(part, arrived.at[d], send_h.at[d], recv_h.at[d], hour=lax.rem(me + d, n))

    for d in hour_peers(n):
        copy(d).start()
    arrived[0] = part[...]
    for d in hour_peers(n):
        copy(d).wait()
    return jnp.sum(arrived[...], axis=0)


def greet_hours(n):
    hour = lax.axis_index("hour")
    return greet("hour", [lax.rem(hour + d, n) for d in hour_peers(n)])


def first_kernel(n, in_ref, place_ref, prof_ref, out_ref, got, acc, square, part, arrived, *sems):
    me = lax.axis_index("samp")
    z, y = me // NY, lax.rem(me, NY)
    count = greet("samp", near_peers(z, y)) + greet_hours(n)
    pl.semaphore_wait(pltpu.get_barrier_semaphore(), count)
    gather_body(spread_into(acc, square, got, place_ref), in_ref, got, *sems[:4])
    fold(acc, square, prof_ref, part)
    out_ref[...] = hour_body(n, part, arrived, *sems[4:])


def vmem(count):
    return [pl.BlockSpec(memory_space=pltpu.VMEM)] * count


def gather_sems():
    dma = pltpu.SemaphoreType.DMA
    return [dma((NY,)), dma((NY,)), dma((2, UP, NY)), dma((2, UP, NY))]


def spread_scratch(n, width, uses):
    part = (uses * width // 128 + 8, 128)
    return [
        pltpu.VMEM((NY * NZ, PAD, 128), jnp.float32),
        pltpu.VMEM((256, width), jnp.float32),
        pltpu.VMEM((8, 128), jnp.float32),
        pltpu.VMEM(part, jnp.float32),
        pltpu.VMEM((n, *part), jnp.float32),
    ]


def first_total(rows, place, profiles, number):
    n = lax.axis_size("hour")
    uses, _, width = profiles.shape
    dma = pltpu.SemaphoreType.DMA
    return pl.pallas_call(
        lambda *refs: first_kernel(n, *refs),
        out_shape=jax.ShapeDtypeStruct((uses * width // 128 + 8, 128), jnp.float32),
        in_specs=vmem(3),
        out_specs=vmem(1)[0],
        scratch_shapes=[*spread_scratch(n, width, uses), *gather_sems(), dma((n,)), dma((n,))],
        compiler_params=pltpu.CompilerParams(collective_id=number, has_side_effects=True),
    )(rows, place, profiles)


def scatter_body(in_ref, out_ref, held, total, arrived, send_y, recv_y, send_z, recv_z):
    me = lax.axis_index("samp")
    z, y = me // NY, lax.rem(me, NY)
    order = (2, 1, 3, 0)

    def z_copy(way, k, j, own=False):
        step = 1 - 2 * way
        far = (UP, DOWN)[way] - k
        src = in_ref.at[at_place(z + step * far, y + j)] if own else held.at[way, k - 1, j]
        return remote(
            src, held.at[way, k, j], send_z.at[way, k, j], recv_z.at[way, k, j],
            samp=at_place(z + step, y),
        )

    def z_arrival(way, k, j):
        step = 1 - 2 * way
        slot = held.at[way, k, j]
        return remote(slot, slot, send_z.at[way, k, j], recv_z.at[way, k, j], samp=at_place(z + step, y))

    def add_own(way, k, j):
        step = 1 - 2 * way
        far = (UP, DOWN)[way] - k
        z_arrival(way, k - 1, j).wait_recv()
        held[way, k - 1, j] = held[way, k - 1, j] + in_ref[at_place(z + step * far, y + j)]
        z_copy(way, k, j).start()

    def y_copy(d):
        return remote(total.at[d], arrived.at[d], send_y.at[d], recv_y.at[d], samp=at_place(z, y + d))

    for j in order:
        for way in (0, 1):
            z_copy(way, 0, j, True).start()

    def hop(k, carry):
        for j in order:
            for way in (0, 1):
                add_own(way, k, j)
        return carry

    lax.fori_loop(1, DOWN, hop, 0)
    for j in order:
        add_own(0, UP - 1, j)
    for j in order:
        z_arrival(1, DOWN - 1, j).wait_recv()
        z_arrival(0, UP - 1, j).wait_recv()
        total[j] = held[0, UP - 1, j] + held[1, DOWN - 1, j] + in_ref[at_place(z, y + j)]
        if j:
            y_copy(j).start()

    def drain(k, carry):
        for j in order:
            for way in (0, 1):
                z_copy(way, k, j).wait_send()
        return carry

    for j in order:
        for way in (0, 1):
            z_copy(way, 0, j, True).wait_send()
    lax.fori_loop(1, DOWN, drain, 0)
    for j in order:
        z_copy(0, UP - 1, j).wait_send()
    for d in (1, 3, 2):
        y_copy(d).wait()
    out_ref[...] = total[0] + arrived[1] + arrived[2] + arrived[3]


def second_kernel(
    n, sample_count, space_count, real,
    in_ref, gap_ref, beta_ref, image_ref, place_ref, prof_ref, load_ref, step_ref, dir_ref,
    kept, got, acc, square, part, arrived, owned, fresh, held, total, landed, first, middle, second, start,
    *sems,
):
    me = lax.axis_index("samp")
    z, y = me // NY, lax.rem(me, NY)
    far_first = sorted(range(1, NZ), key=lambda d: -min(d, NZ - d))
    rows = image_ref.shape[0]
    send_y, recv_y, send_z, recv_z = sems[10:]

    def y_copy(d):
        return remote(start, first.at[d], send_y.at[d], recv_y.at[d], samp=at_place(z, y + d))

    def z_copy(d):
        return remote(middle, second.at[d], send_z.at[d], recv_z.at[d], samp=at_place(z + d, y))

    peers = [at_place(z + d, y) for d in far_first] + [at_place(z, y + d) for d in (2, 1, 3)]
    count = greet("samp", peers) + greet_hours(n)
    pl.semaphore_wait(pltpu.get_barrier_semaphore(), count)
    scatter_body(in_ref, owned, held, total, landed, *sems[:4])
    alpha_one = jnp.sqrt(owned[pl.ds(real, 1)] / sample_count + epsilon)
    beta_one = beta_ref[pl.ds(0, 1)]
    mismatch = owned[...] / alpha_one - (alpha_one / beta_one) * gap_ref[...]
    row = lax.broadcasted_iota(jnp.int32, mismatch.shape, 0)
    mismatch = jnp.where(row < real, mismatch, 0.0)
    fresh[...] = mismatch
    gather_body(spread_into(acc, square, got, place_ref), fresh, got, *sems[4:8])
    fold(acc, square, prof_ref, part)
    whole = hour_body(n, part, arrived, *sems[8:10])
    beta_two = jnp.sqrt(whole[rows:rows + 1] / space_count + epsilon)
    image_two = whole[:rows] / beta_two - beta_two * (image_ref[...] / alpha_one)
    kept[...] = image_two
    load_ref[...] = mismatch / beta_two
    start[...] = jnp.full(start.shape, jnp.sum(image_two * image_two))
    for d in (2, 1, 3):
        y_copy(d).start()
    first[0] = start[...]
    for d in (1, 3, 2):
        y_copy(d).wait()
    middle[...] = jnp.sum(first[...], axis=0)
    for d in far_first:
        z_copy(d).start()
    second[0] = middle[...]
    for d in far_first[::-1]:
        z_copy(d).wait()
    alpha_two = jnp.sqrt(jnp.sum(second[...], axis=0)[:1] / sample_count + epsilon)
    rho_value = jnp.sqrt(alpha_one * alpha_one + beta_two * beta_two)
    cosine = alpha_one / rho_value
    sine = beta_two / rho_value
    uses = prof_ref.shape[0]
    each = rows // uses
    share = each // n
    for e in range(uses):
        spot = pl.ds(e * each + lax.axis_index("hour") * share, share)
        vector_one = image_ref[spot] / alpha_one
        step_ref[pl.ds(e * share, share)] = cosine * beta_one / rho_value * vector_one
        dir_ref[pl.ds(e * share, share)] = (
            kept[spot] / alpha_two - sine * alpha_two / rho_value * vector_one
        )


def second_totals(sums, gap, beta, image, place, profiles, sample_count, space_count, real, number):
    n = lax.axis_size("hour")
    uses, _, width = profiles.shape
    block, small = sums.shape[1:], (8, 128)
    dma = pltpu.SemaphoreType.DMA
    return pl.pallas_call(
        lambda *refs: second_kernel(n, sample_count, space_count, real, *refs),
        out_shape=[
            jax.ShapeDtypeStruct(block, jnp.float32),
            jax.ShapeDtypeStruct((image.shape[0] // n, 128), jnp.float32),
            jax.ShapeDtypeStruct((image.shape[0] // n, 128), jnp.float32),
        ],
        in_specs=vmem(6),
        out_specs=vmem(3),
        scratch_shapes=[
            pltpu.VMEM(image.shape, jnp.float32),
            *spread_scratch(n, width, uses),
            pltpu.VMEM(block, jnp.float32),
            pltpu.VMEM(block, jnp.float32),
            pltpu.VMEM((2, UP, NY, *block), jnp.float32),
            pltpu.VMEM((NY, *block), jnp.float32),
            pltpu.VMEM((NY, *block), jnp.float32),
            pltpu.VMEM((NY, *small), jnp.float32),
            pltpu.VMEM(small, jnp.float32),
            pltpu.VMEM((NZ, *small), jnp.float32),
            pltpu.VMEM(small, jnp.float32),
            *gather_sems(), *gather_sems(), dma((n,)), dma((n,)),
            dma((NY,)), dma((NY,)), dma((NZ,)), dma((NZ,)),
        ],
        compiler_params=pltpu.CompilerParams(collective_id=number, has_side_effects=True),
    )(sums, gap, beta, image, place, profiles)


def two_pieces(x, axis):
    high = lax.reduce_precision(x, 8, 7)
    return jnp.concatenate([high, x - high], axis=axis).astype(jnp.bfloat16)


def local(load_gap, profiles, slot_of_sample, slot_county):
    owners = lax.axis_size("samp")
    hour_count = lax.axis_size("hour")
    owner_index = lax.axis_index("samp")
    use_count, hour_dev, samp_dev = profiles.shape
    per_owner = load_gap.shape[0]
    row_width = use_count * hour_dev
    share_len = samp_dev // hour_count
    space_count = float(per_owner * owners * row_width * hour_count)
    sample_count = float(use_count * samp_dev * owners)
    my_counties = lax.dynamic_index_in_dim(slot_county, owner_index, 0, keepdims=False)
    slots = jnp.arange(slot_county.shape[1], dtype=jnp.int32)
    county = jnp.sum(
        jnp.where(slots[:, None] == slot_of_sample[None, :], my_counties[:, None], 0), axis=0
    )
    place = county // per_owner * PAD + county % per_owner
    places = jnp.arange(owners * PAD, dtype=jnp.int32)
    onehot = (places[:, None] == place[None, :]).astype(jnp.bfloat16)
    wide = profiles.astype(jnp.float32)

    def padded(rows):
        return jnp.pad(rows, ((0, PAD - per_owner), (0, 0)))

    gap_rows = load_gap.reshape(per_owner, row_width)
    total = first_total(padded(gap_rows), place[None], profiles, 1)
    plain, gap_total = total[:-8].reshape(use_count, samp_dev), total[-1, 0]
    beta_one = jnp.sqrt(gap_total / space_count + epsilon)
    image = plain / beta_one
    weighted = (wide * image[:, None, :]).reshape(row_width, samp_dev)
    sums = lax.dot_general(
        onehot, two_pieces(weighted, 0), (((1,), (1,)), ((), ())), preferred_element_type=jnp.float32
    )
    sums = (sums[:, :row_width] + sums[:, row_width:]).reshape(owners, PAD, row_width)
    mine = jnp.sum(image * image)
    row = jnp.arange(PAD, dtype=jnp.int32)[None, :, None]
    sums = jnp.where(row == per_owner, mine, sums)
    load_dir, weight_step, search_dir = second_totals(
        sums, padded(gap_rows), jnp.full((8, 128), beta_one), total[:-8] / beta_one, place[None],
        profiles, sample_count, space_count, per_owner, 2,
    )
    return (
        weight_step.reshape(use_count, share_len),
        search_dir.reshape(use_count, share_len),
        load_dir[:per_owner].reshape(per_owner, use_count, hour_dev),
    )


def solution(mesh):
    return jax.shard_map(
        local,
        mesh=mesh,
        in_specs=(P("samp", None, "hour"), P(None, "hour", "samp"), P("samp"), P()),
        out_specs=(P(None, ("samp", "hour")), P(None, ("samp", "hour")), P("samp", None, "hour")),
        check_vma=False,
    )
```
